128 devices in a mesh: dom: 16 (over y, z), sub: 8 (over x, core).
Axes of the slice: x: 4, y: 4, z: 4, core: 2. Of those that a mesh axis runs over, the one named last changes fastest.
Arguments:
- pos_vel: float32 [32768, 6, 128], P(('dom', 'sub')), may hold values from -6 to 6
- entropy: float32 [32768, 128], P(('dom', 'sub')), may hold values from 0.5 to 4
- masses: float32 [32768, 128], P(('dom', 'sub')), may hold values from 0.5 to 2
- destination: int32 [32768], P(('dom', 'sub')), may hold values from 0 to 127, as said below
- ghost_send: int32 [2, 16384], P(None, ('dom', 'sub')), may hold values from 0 to 255
- pair_list: int32 [2, 32768, 2], P(None, ('dom', 'sub')), may hold values from 0 to 383
Outputs:
- final_state: float32 [32768, 6, 128], P(('dom', 'sub'))
- density: float32 [32768, 128], P(('dom', 'sub'))
The draws below stay inside these ranges and needn't reach their ends.
Inputs may be any that keep to these rules, and one draw needn't show every extreme that they name: `destination`: each device sends exactly 128 of its blocks to other devices and keeps the rest, so it also receives exactly 128. The number of blocks that device s sends to device (s + k) modulo the device count depends only on k, is at most 2, and equals 2 for some k.
All inputs are finite; a program needn't handle non-finite values.
Results may differ from the reference program's by a relative error of at most 0.0001.
Values sent between devices are 32-bit elements; how exact they have to be, the bound alone decides.
A program may use at most 64 MiB of HBM per device.

```python
import math
import jax
import jax.numpy as jnp
from jax import lax

NB = 256
BS = 128
GH = 64
KN = 2
STEPS = 2
TOTAL = 32768
N_DOM = 16
N_SUB = 8


def draw_destination(key, part):
    dev_count = TOTAL // NB
    key_perm, key_twos, key_blocks = jax.random.split(jax.random.fold_in(key, 11), 3)
    shifts = (jax.random.permutation(key_perm, dev_count - 1) + 1).astype(jnp.int32)
    doubled = jax.random.randint(key_twos, (), 1, dev_count // 4 + 1)
    position = jnp.arange(dev_count - 1, dtype=jnp.int32)
    repeats = jnp.where(position < doubled, 2, jnp.where(position < 2 * doubled - 1, 0, 1))
    moves = jnp.repeat(shifts, repeats, total_repeat_length=dev_count).astype(jnp.int32)
    padded = jnp.concatenate([moves, jnp.zeros((NB - dev_count,), jnp.int32)])

    def one_device(device_key, device):
        shuffled = jax.random.permutation(device_key, NB).astype(jnp.int32)
        return jnp.zeros((NB,), jnp.int32).at[shuffled].set((device + padded) % dev_count)
    device_keys = jax.random.split(key_blocks, dev_count)
    return jax.vmap(one_device)(device_keys, jnp.arange(dev_count, dtype=jnp.int32)).reshape(-1).astype(jnp.int32)


def set_ends(array, own_key, low, largest):
    place = [jax.random.randint(jax.random.fold_in(own_key, axis), (), 0, length) for axis, length in enumerate(array.shape)]
    longest = array.shape.index(max(array.shape))
    next_to = place[:longest] + [(place[longest] + 1) % array.shape[longest]] + place[longest + 1:]
    return array.at[tuple(place)].set(low).at[tuple(next_to)].set(largest)


def block_levels(stream_key, dims, shards, low, top_value):
    gain, own = 1.0, jax.random.fold_in(stream_key, 6)
    for axis_at, blocks in shards:
        steps = jnp.exp(jax.random.uniform(jax.random.fold_in(own, axis_at), (blocks,), jnp.float32, low / len(shards), top_value / len(shards)))
        gain = gain * jnp.repeat(steps, dims[axis_at] // blocks).reshape([-1 if axis == axis_at else 1 for axis in range(len(dims))])
    return gain


def bell_draw(stream_key, shape, deviation, reach, pieces=(), held_as=jnp.bfloat16):
    gain = block_levels(stream_key, shape, pieces, -0.22, 0.18) if pieces else 1.0
    array = jax.random.normal(stream_key, shape, jnp.float32) * deviation * gain
    return jnp.minimum(jnp.maximum(array, -reach), reach).astype(held_as)


def setup_inputs(seed: int = 0) -> dict:
    key_list = jax.random.split(jax.random.key(seed), 7)
    pos_vel = bell_draw(key_list[0], (TOTAL, 6, BS), 1.0, 6.0, ((0, 128),), jnp.float32)
    entropy = jnp.clip(jnp.exp(math.log(4.0) - 2.0794415 * jax.random.uniform(key_list[1], (TOTAL, BS), jnp.float32) ** block_levels(key_list[1], (TOTAL, BS), ((0, 128),), -0.2, 0.2)), 0.5, 4.0)
    masses = jnp.clip(jnp.exp(math.log(2.0) - 1.3862944 * jax.random.uniform(key_list[2], (TOTAL, BS), jnp.float32) ** block_levels(key_list[2], (TOTAL, BS), ((0, 128),), -0.2, 0.2)), 0.5, 2.0)
    destination = draw_destination(jax.random.fold_in(key_list[6], 71), 0)
    ghost_send = set_ends(jax.random.randint(key_list[4], (STEPS, 2 * GH * N_DOM * N_SUB), 0, NB), jax.random.fold_in(key_list[4], 1), 0, NB - 1).astype(jnp.int32)
    pair_list = set_ends(jax.random.randint(key_list[5], (STEPS, TOTAL, KN), 0, NB + 2 * GH), jax.random.fold_in(key_list[5], 1), 0, (NB + 2 * GH) - 1).astype(jnp.int32)
    return dict(pos_vel=pos_vel, entropy=entropy, masses=masses, destination=destination, ghost_send=ghost_send, pair_list=pair_list)


time_step = 0.25
group_rows = 32


def interact(near_block, far_block, near_press, far_press):
    diff_x = near_block[:, 0, :, None] - far_block[:, 0, None, :]
    diff_y = near_block[:, 1, :, None] - far_block[:, 1, None, :]
    diff_z = near_block[:, 2, :, None] - far_block[:, 2, None, :]
    kernel = jnp.exp(-0.5 * (diff_x * diff_x + diff_y * diff_y + diff_z * diff_z))
    near_mass = near_block[:, 3, :, None]
    far_mass = far_block[:, 3, None, :]
    if near_press is None:
        to_self = jnp.sum(kernel * far_mass, axis=2)[:, None, :]
        to_other = jnp.sum(kernel * near_mass, axis=1)[:, None, :]
        return to_self, to_other
    coupling = kernel * near_mass * far_mass * (near_press[:, :, None] + far_press[:, None, :])
    to_self = jnp.stack([jnp.sum(coupling * diff_x, axis=2), jnp.sum(coupling * diff_y, axis=2), jnp.sum(coupling * diff_z, axis=2)], axis=1)
    to_other = -jnp.stack([jnp.sum(coupling * diff_x, axis=1), jnp.sum(coupling * diff_y, axis=1), jnp.sum(coupling * diff_z, axis=1)], axis=1)
    return to_self, to_other


def pair_pass(combined, listed, pressure):
    local_count = listed.shape[0]
    columns = listed.shape[1]
    rows_out = 1 if pressure is None else 3
    totals = jnp.zeros((combined.shape[0], rows_out, combined.shape[2]), jnp.float32)

    def one_group(group_index, totals):
        first_row = group_index * group_rows
        leaf_block = lax.dynamic_slice_in_dim(combined, first_row, group_rows, 0)
        partners = lax.dynamic_slice_in_dim(listed, first_row, group_rows, 0)
        near_press = None if pressure is None else lax.dynamic_slice_in_dim(pressure, first_row, group_rows, 0)
        own_sum, unused = interact(leaf_block, leaf_block, near_press, near_press)
        for column in range(columns):
            target = partners[:, column]
            partner = combined[target]
            far_press = None if pressure is None else pressure[target]
            to_self, to_other = interact(leaf_block, partner, near_press, far_press)
            own_sum = own_sum + to_self
            totals = totals.at[target].add(to_other)
        current = lax.dynamic_slice_in_dim(totals, first_row, group_rows, 0)
        return lax.dynamic_update_slice_in_dim(totals, current + own_sum, first_row, 0)

    return lax.fori_loop(0, local_count // group_rows, one_group, totals)


def neighbours(picked):
    zero_rim = jnp.zeros_like(picked[:1, :, :GH])
    from_left = jnp.concatenate([zero_rim, picked[:-1, :, GH:]], 0)
    from_right = jnp.concatenate([picked[1:, :, :GH], zero_rim], 0)
    return jnp.concatenate([from_left, from_right], 2)


def spread(values):
    devices_all = N_DOM * N_SUB
    return neighbours(values.reshape((N_DOM, N_SUB) + values.shape[1:])).reshape((devices_all,) + values.shape[1:])


def gather_back(partials, send_rows):
    incoming = spread(partials[:, NB:])
    return jax.vmap(lambda local_part, indices, returned: local_part.at[indices].add(returned))(partials[:, :NB], send_rows, incoming)


def reference(pos_vel, entropy, masses, destination, ghost_send, pair_list):
    devices_all = N_DOM * N_SUB
    serial = jnp.arange(TOTAL, dtype=jnp.int32)
    anchor = serial // NB
    moving = (destination != anchor).astype(jnp.int32)
    sort_key = destination * (2 * TOTAL) + moving * TOTAL + serial
    new_order = jnp.argsort(sort_key).astype(jnp.int32)
    particle = pos_vel[new_order].reshape(devices_all, NB, 6, BS)
    entropy_dev = entropy[new_order].reshape(devices_all, NB, BS)
    mass_dev = masses[new_order].reshape(devices_all, NB, BS)
    pick = jax.vmap(lambda values, indices: values[indices])
    density = jnp.zeros((devices_all, NB, 1, BS), jnp.float32)
    for section_index in range(STEPS):
        send_rows = ghost_send[section_index].reshape(devices_all, 2 * GH)
        listed = pair_list[section_index].reshape(devices_all, NB, KN)
        physical = jnp.concatenate([particle[:, :, 0:3], mass_dev[:, :, None]], 2)
        ghosts = spread(pick(physical, send_rows))
        combined = jnp.concatenate([physical, ghosts], 1)
        partial_rho = lax.map(lambda member: pair_pass(member[0], member[1], None), (combined, listed))
        density = gather_back(partial_rho, send_rows)
        pressure = entropy_dev * density[:, :, 0] ** (-1.0 / 3.0)
        ghost_press = spread(pick(pressure, send_rows))
        press_all = jnp.concatenate([pressure, ghost_press], 1)
        partial_force = lax.map(lambda member: pair_pass(member[0], member[1], member[2]), (combined, listed, press_all))
        force_sum = gather_back(partial_force, send_rows)
        velocity = particle[:, :, 3:6] + time_step * force_sum / mass_dev[:, :, None]
        position = particle[:, :, 0:3] + time_step * velocity
        particle = jnp.concatenate([position, velocity], 2)
    return particle.reshape(TOTAL, 6, BS), density[:, :, 0].reshape(TOTAL, BS)
```

```python
import math

import jax
import jax.numpy as jnp
from jax import lax
from jax.experimental import pallas as pl
from jax.experimental.pallas import tpu as pltpu
from jax.sharding import PartitionSpec as P

f32, bf16 = jnp.float32, jnp.bfloat16
SCALE = math.sqrt(math.log2(math.e))


def rounded(x):
    return x.astype(bf16).astype(f32)


def split3(x):
    high = rounded(x)
    rest = x - high
    mid = rounded(rest)
    return high, mid, rest - mid


def split2(x):
    high = x.astype(bf16)
    return high, (x - high.astype(f32)).astype(bf16)


def features(block, centre, row):
    moved = block - centre
    square = jnp.where(row < 3, moved * moved, 0.0)
    half = 0.5 * jnp.sum(square, axis=0, keepdims=True)
    return jnp.where((row == 3) | (row == 4), moved - half, moved)


def left_rows(moved, row):
    h, m, l = split3(moved)
    one = jnp.where(row == 4, 1.0, 0.0)
    a1 = jnp.where(row < 4, h, one)
    a2 = jnp.where(row < 3, h, jnp.where(row == 3, m, one))
    a3 = jnp.where(row < 3, m, jnp.where(row == 3, l, one))
    a4 = jnp.where(row < 3, m, 0.0)
    a5 = jnp.where(row < 3, h, 0.0)
    a6 = jnp.where(row < 3, l, 0.0)
    return jnp.concatenate([a1, a2, a3, a4, a5, a6], 0).astype(bf16)


def right_rows(moved, row):
    h, m, l = split3(moved)
    one = jnp.where(row == 3, 1.0, 0.0)
    low = row < 3
    four = row == 4
    b1 = jnp.where(low | four, h, one)
    b2 = jnp.where(low | four, m, one)
    b3 = jnp.where(low, h, jnp.where(four, l, one))
    b4 = jnp.where(low, m, 0.0)
    b5 = jnp.where(low, l, 0.0)
    b6 = jnp.where(low, h, 0.0)
    return jnp.concatenate([b1, b2, b3, b4, b5, b6], 0).astype(bf16)


def centre_of(block, row):
    return jnp.where(row < 3, jnp.mean(block, axis=1, keepdims=True), 0.0)


def weights_of(own, first, second, row):
    left = left_rows(own, row)
    right = jnp.concatenate(
        [right_rows(own, row), right_rows(first, row), right_rows(second, row)], 1
    )
    exponent = lax.dot_general(
        left, right, (((0,), (0,)), ((), ())), preferred_element_type=f32
    )
    return jnp.exp2(exponent)


def fold(x):
    return jnp.sum(x.reshape(-1, 8, x.shape[-1]), 0)


MOST = 2
STEP = 0.25
UNROLL = 16
GHOSTS = 64


def each(count, body, unroll=8):
    def group(g, _):
        for u in range(unroll):
            body(g * unroll + u)
        return 0

    lax.fori_loop(0, count // unroll, group, 0)


def build_blocks(state, low, high, blocks):
    local = state.shape[0]

    def rows(x, m):
        level = jnp.where(m > 0.0, jnp.log2(jnp.maximum(m, 1e-30)), -300.0)
        return jnp.concatenate([x * SCALE, level, level, jnp.zeros_like(x)], 1)

    def own(g):
        part = state[pl.ds(g * 8, 8)]
        blocks[pl.ds(g * 8, 8)] = rows(part[:, 0:3], part[:, 7:8])

    each(local // 8, own, 4)
    for start, side in ((local, low), (local + GHOSTS, high)):
        def ghost(g, start=start, side=side):
            part = side[pl.ds(g * 8, 8)]
            blocks[pl.ds(start + g * 8, 8)] = rows(part[:, 0:3], part[:, 3:4])

        each(GHOSTS // 8, ghost, 4)


def density_kernel(pairs, state, low, high, local_out, low_out, high_out, blocks, sums):
    local = state.shape[0]
    build_blocks(state, low, high, blocks)
    sums[...] = jnp.zeros_like(sums)
    row = lax.broadcasted_iota(jnp.int32, (8, 128), 0)

    def one(i):
        n1, n2 = pairs[2 * i], pairs[2 * i + 1]
        own = blocks[i]
        centre = centre_of(own, row)
        own, first, second = (
            features(b, centre, row) for b in (own, blocks[n1], blocks[n2])
        )
        m = weights_of(own, first, second, row)
        back = (m[:, 128:256] + m[:, 256:384]).T
        sums[n1] += fold(m[:, 128:256])
        sums[n2] += fold(m[:, 256:384])
        sums[i] += fold(m[:, 0:128]) + fold(back)

    each(local, one, UNROLL)
    for start, count, out in ((0, local, local_out), (local, GHOSTS, low_out), (local + GHOSTS, GHOSTS, high_out)):
        out[...] = jnp.sum(sums[start : start + count], axis=1, keepdims=True)


def pressure_kernel(send, state, own, low, high, density, press, low_pick, high_pick, total):
    total[...] = own[...]

    def back(j):
        total[send[j]] += low[j]

    def back_high(j):
        total[send[GHOSTS + j]] += high[j]

    each(GHOSTS, back)
    each(GHOSTS, back_high)
    rho = total[...] / state[:, 7:8, :]
    density[...] = rho
    press[...] = state[:, 6:7, :] * jnp.exp2(jnp.log2(rho) * (-1.0 / 3.0))

    def pick(j):
        low_pick[j] = press[send[j]]
        high_pick[j] = press[send[GHOSTS + j]]

    each(GHOSTS, pick)


def force_rows(v, y):
    x, qx, q = v[0:3], v[3:6], v[6:7]
    return qx * y[7:8] + x * y[6:7] - q * y[0:3] - y[3:6]


def vector_rows(moved, q):
    x = moved[0:3]
    return jnp.concatenate([x, x * q, q, jnp.ones_like(q)], 0)


def force_kernel(pairs, state, low, high, press_own, press_low, press_high, local_out, low_out, high_out, blocks, press, force):
    local = state.shape[0]
    build_blocks(state, low, high, blocks)
    press[0:local] = press_own[...]
    press[local : local + GHOSTS] = press_low[...]
    press[local + GHOSTS :] = press_high[...]
    force[...] = jnp.zeros_like(force)
    row = lax.broadcasted_iota(jnp.int32, (8, 128), 0)
    zero = jnp.zeros((5, 128), f32)
    dims = (((1,), (1,)), ((), ()))

    def one(i):
        n1, n2 = pairs[2 * i], pairs[2 * i + 1]
        own = blocks[i]
        centre = centre_of(own, row)
        own, first, second = (
            features(b, centre, row) for b in (own, blocks[n1], blocks[n2])
        )
        m = weights_of(own, first, second, row)
        mh, ml = split2(m)
        vs = [vector_rows(b, press[n]) for b, n in ((own, i), (first, n1), (second, n2))]
        vv = [jnp.concatenate(split2(v), 0) for v in vs]
        v_all = jnp.concatenate(vv, 1)
        across = lax.dot_general(
            jnp.concatenate([mh, ml], 1), jnp.concatenate([v_all, v_all], 1), dims,
            preferred_element_type=f32,
        ).T
        across = across[0:8] + across[8:16]
        stacked = jnp.concatenate([mh[:, 128:], ml[:, 128:]], 0)
        down = jnp.dot(
            jnp.concatenate([vv[0], vv[0]], 1), stacked, preferred_element_type=f32
        )
        down = down[0:8] + down[8:16]
        for n, v, y in ((n1, vs[1], down[:, :128]), (n2, vs[2], down[:, 128:]), (i, vs[0], across)):
            force[n] += jnp.concatenate([force_rows(v, y), zero], 0)

    each(local, one, 8)
    for start, count, out in ((0, local, local_out), (local, GHOSTS, low_out), (local + GHOSTS, GHOSTS, high_out)):
        out[...] = force[start : start + count, 0:3, :] * (1.0 / SCALE)


def picks(send, state, low_pick, high_pick):
    def pick(j):
        for side, out in ((0, low_pick), (GHOSTS, high_pick)):
            block = state[send[side + j]]
            out[j] = jnp.concatenate([block[0:3], block[7:8]], 0)

    each(GHOSTS, pick)


def moved_state(send, state, own, low, high, total):
    total[...] = own[...]

    def back(j):
        total[send[j]] += low[j]

    def back_high(j):
        total[send[GHOSTS + j]] += high[j]

    each(GHOSTS, back)
    each(GHOSTS, back_high)
    velocity = state[:, 3:6, :] + STEP * total[...] / state[:, 7:8, :]
    return state[:, 0:3, :] + STEP * velocity, velocity


def move_kernel(send, send_next, state, own, low, high, new, low_pick, high_pick, total):
    position, velocity = moved_state(send, state, own, low, high, total)
    new[:, 0:3, :] = position
    new[:, 3:6, :] = velocity
    new[:, 6:8, :] = state[:, 6:8, :]
    picks(send_next, new, low_pick, high_pick)


def last_kernel(send, state, own, low, high, new, total):
    position, velocity = moved_state(send, state, own, low, high, total)
    new[:, 0:3, :] = position
    new[:, 3:6, :] = velocity


def pack_kernel(index, pos_vel, entropy, masses, packed, outbox):
    packed[:, 0:6, :] = pos_vel[...]
    packed[:, 6:7, :] = entropy[...]
    packed[:, 7:8, :] = masses[...]

    def one(j):
        outbox[j] = packed[index[j]]

    each(outbox.shape[0], one)


def place_kernel(index, send, packed, arrived, state, low_pick, high_pick):
    half = state.shape[0] // 2

    def stay(j):
        state[j] = packed[index[j]]

    def come(j):
        state[half + j] = arrived[index[half + j]]

    each(half, stay)
    each(half, come)
    picks(send, state, low_pick, high_pick)


def call(kernel, name, scalars, operands, outs, scratch=()):
    vmem, smem = (pl.BlockSpec(memory_space=s) for s in (pltpu.VMEM, pltpu.SMEM))
    return pl.pallas_call(
        kernel,
        name=name,
        out_shape=[jax.ShapeDtypeStruct(s, f32) for s in outs],
        in_specs=[smem] * len(scalars) + [vmem] * len(operands),
        out_specs=[vmem] * len(outs),
        scratch_shapes=[pltpu.VMEM(s, f32) for s in scratch],
    )(*scalars, *operands)


def swap(low, high):
    count = lax.axis_size("dom")
    up = [(i, i + 1) for i in range(count - 1)]
    down = [(j, i) for i, j in up]
    return lax.ppermute(high, "dom", up), lax.ppermute(low, "dom", down)


def shards(pos_vel, entropy, masses, destination, ghost_send, pair_list):
    devices = lax.axis_size(("dom", "sub"))
    me = lax.axis_index(("dom", "sub"))
    local = pos_vel.shape[0]
    size = pos_vel.shape[2]
    number = jnp.arange(local, dtype=jnp.int32)
    device = jnp.arange(devices, dtype=jnp.int32)
    slot = jnp.arange(devices * MOST, dtype=jnp.int32)
    same = destination[:, None] == destination[None, :]
    rank = jnp.sum((same & (number[:, None] < number[None, :])).astype(jnp.int32), 0)
    staying = destination == me
    out_slot = jnp.where(staying, -1, destination * MOST + rank)
    pack_index = jnp.sum(jnp.where(out_slot[:, None] == slot[None, :], number[:, None], 0), 0)
    shift = (destination - me) % devices
    wanted = (me - device) % devices
    come = jnp.sum((shift[:, None] == wanted[None, :]).astype(jnp.int32), 0)
    come = jnp.where(device == me, 0, come)
    before = jnp.sum(jnp.where(device[:, None] < device[None, :], come[:, None], 0), 0)
    turn = slot % MOST
    source = slot // MOST
    come_at = source[:, None] == device[None, :]
    first = jnp.sum(jnp.where(come_at, before[None, :], 0), 1)
    many = jnp.sum(jnp.where(come_at, come[None, :], 0), 1)
    place = jnp.where(turn < many, first + turn, -1)
    half = local - devices
    stay_index = jnp.sum(
        jnp.where(staying[:, None] & (rank[:, None] == number[None, :half]), number[:, None], 0), 0
    )
    come_index = jnp.sum(jnp.where(place[:, None] == device[None, :], slot[:, None], 0), 0)
    place_index = jnp.concatenate([stay_index, come_index])

    block = (local, 8, size)
    pick4, pick1, pick3 = ((GHOSTS, r, size) for r in (4, 1, 3))
    one, three = (local, 1, size), (local, 3, size)
    total = local + 2 * GHOSTS
    packed, outbox = call(
        pack_kernel, "pack", (pack_index,), (pos_vel, entropy[:, None], masses[:, None]),
        (block, (devices * MOST, 8, size)),
    )
    arrived = lax.all_to_all(
        outbox.reshape(devices, MOST, 8, size), ("dom", "sub"), split_axis=0, concat_axis=0, tiled=True
    ).reshape(devices * MOST, 8, size)
    state, low_pick, high_pick = call(
        place_kernel, "place", (place_index, ghost_send[0]), (packed, arrived), (block, pick4, pick4)
    )
    steps = ghost_send.shape[0]
    for s in range(steps):
        send, pairs = ghost_send[s], pair_list[s].reshape(-1)
        low, high = swap(low_pick, high_pick)
        own, low_back, high_back = call(
            density_kernel, "density", (pairs,), (state, low, high), (one, pick1, pick1),
            ((total, 8, size), (total, 8, size)),
        )
        low_in, high_in = swap(low_back, high_back)
        density, press, low_pick, high_pick = call(
            pressure_kernel, "pressure", (send,), (state, own, low_in, high_in),
            (one, one, pick1, pick1), (one,),
        )
        press_low, press_high = swap(low_pick, high_pick)
        own, low_back, high_back = call(
            force_kernel, "force", (pairs,), (state, low, high, press, press_low, press_high),
            (three, pick3, pick3), ((total, 8, size), (total, 1, size), (total, 8, size)),
        )
        low_in, high_in = swap(low_back, high_back)
        if s + 1 < steps:
            state, low_pick, high_pick = call(
                move_kernel, "move", (send, ghost_send[s + 1]), (state, own, low_in, high_in),
                (block, pick4, pick4), (three,),
            )
        else:
            (state,) = call(
                last_kernel, "last", (send,), (state, own, low_in, high_in), ((local, 6, size),), (three,)
            )
    return state, density[:, 0]


def solution(mesh):
    both = ("dom", "sub")
    in_specs = (P(both, None, None), P(both, None), P(both, None), P(both), P(None, both), P(None, both, None))
    out_specs = (P(both, None, None), P(both, None))
    return jax.shard_map(shards, mesh=mesh, in_specs=in_specs, out_specs=out_specs, check_vma=False)
```

```python
import functools
import math

import jax
import jax.numpy as jnp
from jax import lax
from jax.experimental import pallas as pl
from jax.experimental.pallas import tpu as pltpu
from jax.sharding import PartitionSpec as P

f32, bf16 = jnp.float32, jnp.bfloat16
SCALE = math.sqrt(math.log2(math.e))


def rounded(x):
    return x.astype(bf16).astype(f32)


def split3(x):
    high = rounded(x)
    rest = x - high
    mid = rounded(rest)
    return high, mid, rest - mid


def split2(x):
    high = x.astype(bf16)
    return high, (x - high.astype(f32)).astype(bf16)


def features(block, centre, row):
    moved = block - centre
    square = jnp.where(row < 3, moved * moved, 0.0)
    half = 0.5 * jnp.sum(square, axis=0, keepdims=True)
    return jnp.where((row == 3) | (row == 4), moved - half, moved)


def left_rows(moved, row):
    h, m, l = split3(moved)
    one = jnp.where(row == 4, 1.0, 0.0)
    a1 = jnp.where(row < 4, h, one)
    a2 = jnp.where(row < 3, h, jnp.where(row == 3, m, one))
    a3 = jnp.where(row < 3, m, jnp.where(row == 3, l, one))
    a4 = jnp.where(row < 3, m, 0.0)
    a5 = jnp.where(row < 3, h, 0.0)
    a6 = jnp.where(row < 3, l, 0.0)
    return jnp.concatenate([a1, a2, a3, a4, a5, a6], 0).astype(bf16)


def right_rows(moved, row):
    h, m, l = split3(moved)
    one = jnp.where(row == 3, 1.0, 0.0)
    low = row < 3
    four = row == 4
    b1 = jnp.where(low | four, h, one)
    b2 = jnp.where(low | four, m, one)
    b3 = jnp.where(low, h, jnp.where(four, l, one))
    b4 = jnp.where(low, m, 0.0)
    b5 = jnp.where(low, l, 0.0)
    b6 = jnp.where(low, h, 0.0)
    return jnp.concatenate([b1, b2, b3, b4, b5, b6], 0).astype(bf16)


def centre_of(block, row):
    return jnp.where(row < 3, jnp.mean(block, axis=1, keepdims=True), 0.0)


def weights_of(left, parts, row):
    right = jnp.concatenate([right_rows(p, row) for p in parts], 1)
    exponent = lax.dot_general(
        left_rows(left, row), right, (((0,), (0,)), ((), ())), preferred_element_type=f32
    )
    return jnp.exp2(exponent)


def fold(x):
    return jnp.sum(x.reshape(-1, 8, x.shape[-1]), 0)


MOST = 2
STEP = 0.25
UNROLL = 8
GHOSTS = 64
NONE = -300.0


def each(count, body, unroll=8):
    def group(g, _):
        for u in range(unroll):
            body(g * unroll + u)
        return 0

    lax.fori_loop(0, count // unroll, group, 0)


def column_sum(x):
    return jnp.sum(fold(x), axis=0, keepdims=True)


def force_rows(v, y):
    x, qx, q = v[0:3], v[3:6], v[6:7]
    return qx * y[7:8] + x * y[6:7] - q * y[0:3] - y[3:6]


def vector_rows(moved, q):
    x = moved[0:3]
    return jnp.concatenate([x, x * q, q, jnp.ones_like(q)], 0)


def halves(v):
    return jnp.concatenate(split2(v), 0)


def join(y):
    return y[0:8] + y[8:16]


def lanes(rows):
    return jnp.concatenate([rows[c : c + 1] for c in range(3)], 1)


def routed_sum(chosen, first, rows, values):
    number = lax.broadcasted_iota(jnp.int32, (rows, chosen.shape[1]), 0) + first
    hot = jnp.where(number == chosen, 1.0, 0.0).astype(bf16)
    width = values.shape[1]
    parts = jnp.concatenate(split3(values), 1).astype(bf16)
    out = jnp.dot(hot, parts, preferred_element_type=f32)
    return out[:, :width] + out[:, width : 2 * width] + out[:, 2 * width :]


def step_kernel(
    domains, steps, send, pairs, send_row, pair_row, start, final, density,
    state, blocks, press, entropy, masses, own_m, pair_m, r_own, r_pair, f_own, f_pair, f_sum,
    p_out, p_in, r_out, r_in, q_out, q_in, f_out, f_in, send_sem, recv_sem,
):
    local = start.shape[0]
    total = local + 2 * GHOSTS
    dom = lax.axis_index("dom")
    has_low, has_high = dom > 0, dom < domains - 1
    row = lax.broadcasted_iota(jnp.int32, (8, 128), 0)

    def links(s, phase, out, into):
        def copy(side, target):
            return pltpu.make_async_remote_copy(
                src_ref=out.at[s, side],
                dst_ref=into.at[s, 1 - side],
                send_sem=send_sem.at[s, phase, side],
                recv_sem=recv_sem.at[s, phase, 1 - side],
                device_id={"dom": target},
                device_id_type=pl.DeviceIdType.MESH,
            )

        return copy(0, dom - 1), copy(1, dom + 1)

    def begin(s, phase, out, into):
        to_low, to_high = links(s, phase, out, into)
        pl.when(has_low)(to_low.start)
        pl.when(has_high)(to_high.start)

    def finish(s, phase, out, into):
        to_low, to_high = links(s, phase, out, into)

        @pl.when(has_low)
        def _():
            to_low.wait_send()
            to_high.wait_recv()

        @pl.when(has_high)
        def _():
            to_high.wait_send()
            to_low.wait_recv()

    if domains > 1:
        barrier = pltpu.get_barrier_semaphore()

        def greet(target):
            pl.semaphore_signal(
                barrier, inc=1, device_id={"dom": target}, device_id_type=pl.DeviceIdType.MESH
            )

        pl.when(has_low)(lambda: greet(dom - 1))
        pl.when(has_high)(lambda: greet(dom + 1))

    for side, has in ((0, has_low), (1, has_high)):

        @pl.when(jnp.logical_not(has))
        def _(side=side):
            for s in range(steps):
                p_in[s, side] = jnp.concatenate(
                    [jnp.zeros((GHOSTS, 3, 128), f32), jnp.full((GHOSTS, 1, 128), NONE, f32)], 1
                )
                for into in (r_in, q_in, f_in):
                    into[s, side] = jnp.zeros(into.shape[2:], f32)

    def enter(i):
        block = start[i]
        state[i] = block
        entropy[pl.ds(i, 1), :] = block[6:7]
        masses[pl.ds(i, 1), :] = block[7:8]

    each(local, enter)

    for s in range(steps):

        def scaled(i):
            block = state[i]
            level = jnp.log2(block[7:8])
            blocks[i] = jnp.concatenate(
                [block[0:3] * SCALE, level, level, jnp.zeros((3, 128), f32)], 0
            )

        each(local, scaled)

        def pick(j):
            for side in range(2):
                p_out[s, side, j] = blocks[send[s, side * GHOSTS + j]][0:4]

        each(GHOSTS, pick)
        if s == 0 and domains > 1:
            pl.semaphore_wait(barrier, has_low.astype(jnp.int32) + has_high.astype(jnp.int32))
        if domains > 1:
            begin(s, 0, p_out, p_in)

        def own_density(i):
            block = blocks[i]
            block = features(block, centre_of(block, row), row)
            m = weights_of(block, (block,), row)
            r_own[pl.ds(i, 1), :] = column_sum(m)
            h, l = split2(m)
            own_m[i, 0:128] = h
            own_m[i, 128:256] = l

        each(local, own_density, UNROLL)
        if domains > 1:
            finish(s, 0, p_out, p_in)

        def ghost(j):
            for side in range(2):
                block = p_in[s, side, j]
                blocks[local + side * GHOSTS + j] = jnp.concatenate(
                    [block, block[3:4], jnp.zeros((3, 128), f32)], 0
                )

        each(GHOSTS, ghost)

        def pair_density(i):
            block = blocks[i]
            centre = centre_of(block, row)
            own, first, second = (
                features(b, centre, row)
                for b in (block, blocks[pairs[s, 2 * i]], blocks[pairs[s, 2 * i + 1]])
            )
            m = weights_of(own, (first, second), row)
            sums = column_sum(m)
            r_pair[pl.ds(2 * i, 1), :] = sums[:, :128]
            r_pair[pl.ds(2 * i + 1, 1), :] = sums[:, 128:]
            r_own[pl.ds(i, 1), :] += column_sum((m[:, :128] + m[:, 128:]).T)
            h, l = split2(m)
            pair_m[i, :, 0:256] = h
            pair_m[i, :, 256:512] = l

        each(local, pair_density, UNROLL)
        chosen = pair_row[s]
        sent = send_row[s]
        for side in range(2):
            r_out[s, side] = routed_sum(chosen, local + side * GHOSTS, GHOSTS, r_pair[...])
        for part in range(0, local, 128):
            r_own[part : part + 128] += routed_sum(chosen, part, 128, r_pair[...])
        if domains > 1:
            begin(s, 1, r_out, r_in)
            finish(s, 1, r_out, r_in)
        incoming = jnp.concatenate([r_in[s, 0], r_in[s, 1]], 0)
        rho = (r_own[...] + routed_sum(sent, 0, local, incoming)) / masses[...]
        if s == steps - 1:
            density[...] = rho
        press[0:local] = entropy[...] * jnp.exp2(jnp.log2(rho) * (-1.0 / 3.0))

        def pick_press(j):
            for side in range(2):
                q_out[s, side, pl.ds(j, 1), :] = press[pl.ds(send[s, side * GHOSTS + j], 1), :]

        each(GHOSTS, pick_press)
        if domains > 1:
            begin(s, 2, q_out, q_in)

        def own_force(i):
            block = blocks[i]
            v = vector_rows(block - centre_of(block, row), press[pl.ds(i, 1), :])
            vv = halves(v)
            y = join(
                jnp.dot(jnp.concatenate([vv, vv], 1), own_m[i], preferred_element_type=f32)
            )
            f_own[pl.ds(i, 1), :] = lanes(force_rows(v, y))

        each(local, own_force, UNROLL)
        if domains > 1:
            finish(s, 2, q_out, q_in)
        press[local : local + GHOSTS] = q_in[s, 0]
        press[local + GHOSTS : total] = q_in[s, 1]

        def pair_force(i):
            block = blocks[i]
            centre = centre_of(block, row)
            n1, n2 = pairs[s, 2 * i], pairs[s, 2 * i + 1]
            vs = [
                vector_rows(b - centre, press[pl.ds(n, 1), :])
                for b, n in ((block, i), (blocks[n1], n1), (blocks[n2], n2))
            ]
            own, first, second = (halves(v) for v in vs)
            far = jnp.concatenate([first, second, first, second], 1)
            across = lax.dot_general(
                pair_m[i], far, (((1,), (1,)), ((), ())), preferred_element_type=f32
            ).T
            f_own[pl.ds(i, 1), :] += lanes(force_rows(vs[0], join(across)))
            stacked = jnp.concatenate([pair_m[i, :, 0:256], pair_m[i, :, 256:512]], 0)
            down = join(
                jnp.dot(jnp.concatenate([own, own], 1), stacked, preferred_element_type=f32)
            )
            f_pair[pl.ds(2 * i, 1), :] = lanes(force_rows(vs[1], down[:, :128]))
            f_pair[pl.ds(2 * i + 1, 1), :] = lanes(force_rows(vs[2], down[:, 128:]))

        each(local, pair_force, UNROLL)
        for side in range(2):
            f_out[s, side] = routed_sum(chosen, local + side * GHOSTS, GHOSTS, f_pair[...])
        for part in range(0, local, 128):
            f_own[part : part + 128] += routed_sum(chosen, part, 128, f_pair[...])
        if domains > 1:
            begin(s, 3, f_out, f_in)
            finish(s, 3, f_out, f_in)
        incoming = jnp.concatenate([f_in[s, 0], f_in[s, 1]], 0)
        for part in range(0, local, 128):
            f_sum[part : part + 128] = f_own[part : part + 128] + routed_sum(sent, part, 128, incoming)

        def move(i):
            block = state[i]
            push = f_sum[pl.ds(i, 1), :] * (STEP / SCALE)
            push = jnp.concatenate([push[:, 0:128], push[:, 128:256], push[:, 256:384]], 0)
            velocity = block[3:6] + push / block[7:8]
            position = block[0:3] + STEP * velocity
            if s == steps - 1:
                final[i] = jnp.concatenate([position, velocity], 0)
            else:
                state[i] = jnp.concatenate([position, velocity, block[6:8]], 0)

        each(local, move)


def run_steps(domains, send, pairs, start):
    steps = send.shape[0]
    local = start.shape[0]
    total = local + 2 * GHOSTS
    vmem, smem = (pl.BlockSpec(memory_space=m) for m in (pltpu.VMEM, pltpu.SMEM))
    buffers = []
    for shape in ((GHOSTS, 4, 128), (GHOSTS, 128), (GHOSTS, 128), (GHOSTS, 384)):
        buffers += [pltpu.VMEM((steps, 2) + shape, f32)] * 2
    return pl.pallas_call(
        functools.partial(step_kernel, domains, steps),
        name="steps",
        out_shape=[
            jax.ShapeDtypeStruct((local, 6, 128), f32),
            jax.ShapeDtypeStruct((local, 128), f32),
        ],
        in_specs=[smem, smem, vmem, vmem, vmem],
        out_specs=[vmem, vmem],
        scratch_shapes=[
            pltpu.VMEM((local, 8, 128), f32),
            pltpu.VMEM((total, 8, 128), f32),
            pltpu.VMEM((total, 128), f32),
            pltpu.VMEM((local, 128), f32),
            pltpu.VMEM((local, 128), f32),
            pltpu.VMEM((local, 256, 128), bf16),
            pltpu.VMEM((local, 128, 512), bf16),
            pltpu.VMEM((local, 128), f32),
            pltpu.VMEM((2 * local, 128), f32),
            pltpu.VMEM((local, 384), f32),
            pltpu.VMEM((2 * local, 384), f32),
            pltpu.VMEM((local, 384), f32),
            *buffers,
            pltpu.SemaphoreType.DMA((steps, 4, 2)),
            pltpu.SemaphoreType.DMA((steps, 4, 2)),
        ],
        compiler_params=pltpu.CompilerParams(
            vmem_limit_bytes=67_000_000,
            **(dict(collective_id=1, has_side_effects=True) if domains > 1 else {}),
        ),
    )(send, pairs, send[:, None], pairs[:, None], start)


def pack_kernel(index, pos_vel, entropy, masses, packed, outbox):
    packed[:, 0:6, :] = pos_vel[...]
    packed[:, 6:7, :] = entropy[...]
    packed[:, 7:8, :] = masses[...]

    def one(j):
        outbox[j] = packed[index[j]]

    each(outbox.shape[0], one)


def place_kernel(index, packed, arrived, state):
    half = state.shape[0] // 2

    def stay(j):
        state[j] = packed[index[j]]

    def come(j):
        state[half + j] = arrived[index[half + j]]

    each(half, stay)
    each(half, come)


def call(kernel, name, scalars, operands, outs, scratch=()):
    vmem, smem = (pl.BlockSpec(memory_space=s) for s in (pltpu.VMEM, pltpu.SMEM))
    return pl.pallas_call(
        kernel,
        name=name,
        out_shape=[jax.ShapeDtypeStruct(s, f32) for s in outs],
        in_specs=[smem] * len(scalars) + [vmem] * len(operands),
        out_specs=[vmem] * len(outs),
        scratch_shapes=[pltpu.VMEM(s, f32) for s in scratch],
    )(*scalars, *operands)


def shards(pos_vel, entropy, masses, destination, ghost_send, pair_list):
    devices = lax.axis_size(("dom", "sub"))
    me = lax.axis_index(("dom", "sub"))
    local = pos_vel.shape[0]
    size = pos_vel.shape[2]
    number = jnp.arange(local, dtype=jnp.int32)
    device = jnp.arange(devices, dtype=jnp.int32)
    slot = jnp.arange(devices * MOST, dtype=jnp.int32)
    same = destination[:, None] == destination[None, :]
    rank = jnp.sum((same & (number[:, None] < number[None, :])).astype(jnp.int32), 0)
    staying = destination == me
    out_slot = jnp.where(staying, -1, destination * MOST + rank)
    pack_index = jnp.sum(jnp.where(out_slot[:, None] == slot[None, :], number[:, None], 0), 0)
    shift = (destination - me) % devices
    wanted = (me - device) % devices
    come = jnp.sum((shift[:, None] == wanted[None, :]).astype(jnp.int32), 0)
    come = jnp.where(device == me, 0, come)
    before = jnp.sum(jnp.where(device[:, None] < device[None, :], come[:, None], 0), 0)
    turn = slot % MOST
    source = slot // MOST
    come_at = source[:, None] == device[None, :]
    first = jnp.sum(jnp.where(come_at, before[None, :], 0), 1)
    many = jnp.sum(jnp.where(come_at, come[None, :], 0), 1)
    place = jnp.where(turn < many, first + turn, -1)
    half = local - devices
    stay_index = jnp.sum(
        jnp.where(staying[:, None] & (rank[:, None] == number[None, :half]), number[:, None], 0), 0
    )
    come_index = jnp.sum(jnp.where(place[:, None] == device[None, :], slot[:, None], 0), 0)
    place_index = jnp.concatenate([stay_index, come_index])

    block = (local, 8, size)
    packed, outbox = call(
        pack_kernel, "pack", (pack_index,), (pos_vel, entropy[:, None], masses[:, None]),
        (block, (devices * MOST, 8, size)),
    )
    arrived = lax.all_to_all(
        outbox.reshape(devices, MOST, 8, size), ("dom", "sub"), split_axis=0, concat_axis=0, tiled=True
    ).reshape(devices * MOST, 8, size)
    (state,) = call(place_kernel, "place", (place_index,), (packed, arrived), (block,))
    steps = ghost_send.shape[0]
    return run_steps(lax.axis_size("dom"), ghost_send, pair_list.reshape(steps, -1), state)


def solution(mesh):
    both = ("dom", "sub")
    in_specs = (P(both, None, None), P(both, None), P(both, None), P(both), P(None, both), P(None, both, None))
    out_specs = (P(both, None, None), P(both, None))
    return jax.shard_map(shards, mesh=mesh, in_specs=in_specs, out_specs=out_specs, check_vma=False)
```

```python
import functools
import math

import jax
import jax.numpy as jnp
from jax import lax
from jax.experimental import pallas as pl
from jax.experimental.pallas import tpu as pltpu
from jax.sharding import PartitionSpec as P

f32, bf16 = jnp.float32, jnp.bfloat16
SCALE = math.sqrt(math.log2(math.e))


def rounded(x):
    return x.astype(bf16).astype(f32)


def split3(x):
    high = rounded(x)
    rest = x - high
    mid = rounded(rest)
    return high, mid, rest - mid


def split2(x):
    high = x.astype(bf16)
    return high, (x - high.astype(f32)).astype(bf16)


def features(block, centre, row):
    moved = block - centre
    square = jnp.where(row < 3, moved * moved, 0.0)
    half = 0.5 * jnp.sum(square, axis=0, keepdims=True)
    return jnp.where((row == 3) | (row == 4), moved - half, moved)


def left_rows(moved, row):
    h, m, l = split3(moved)
    one = jnp.where(row == 4, 1.0, 0.0)
    a1 = jnp.where(row < 4, h, one)
    a2 = jnp.where(row < 3, h, jnp.where(row == 3, m, one))
    a3 = jnp.where(row < 3, m, jnp.where(row == 3, l, one))
    a4 = jnp.where(row < 3, m, 0.0)
    a5 = jnp.where(row < 3, h, 0.0)
    a6 = jnp.where(row < 3, l, 0.0)
    return jnp.concatenate([a1, a2, a3, a4, a5, a6], 0).astype(bf16)


def right_rows(moved, row):
    h, m, l = split3(moved)
    one = jnp.where(row == 3, 1.0, 0.0)
    low = row < 3
    four = row == 4
    b1 = jnp.where(low | four, h, one)
    b2 = jnp.where(low | four, m, one)
    b3 = jnp.where(low, h, jnp.where(four, l, one))
    b4 = jnp.where(low, m, 0.0)
    b5 = jnp.where(low, l, 0.0)
    b6 = jnp.where(low, h, 0.0)
    return jnp.concatenate([b1, b2, b3, b4, b5, b6], 0).astype(bf16)


def centre_of(block, row):
    return jnp.where(row < 3, jnp.mean(block, axis=1, keepdims=True), 0.0)


def weights_of(left, parts, row):
    right = jnp.concatenate([right_rows(p, row) for p in parts], 1)
    exponent = lax.dot_general(
        left_rows(left, row), right, (((0,), (0,)), ((), ())), preferred_element_type=f32
    )
    return jnp.exp2(exponent)


def fold(x):
    return jnp.sum(x.reshape(-1, 8, x.shape[-1]), 0)


MOST = 2
STEP = 0.25
UNROLL = 8
GHOSTS = 64
NONE = -300.0


def each(count, body, unroll=8):
    def group(g, _):
        for u in range(unroll):
            body(g * unroll + u)
        return 0

    lax.fori_loop(0, count // unroll, group, 0)


def column_sum(x):
    return jnp.sum(fold(x), axis=0, keepdims=True)


def force_rows(v, y):
    x, qx, q = v[0:3], v[3:6], v[6:7]
    return qx * y[7:8] + x * y[6:7] - q * y[0:3] - y[3:6]


def vector_rows(moved, q):
    x = moved[0:3]
    return jnp.concatenate([x, x * q, q, jnp.ones_like(q)], 0)


def halves(v):
    return jnp.concatenate(split2(v), 0)


def join(y):
    return y[0:8] + y[8:16]


def lanes(rows):
    return jnp.concatenate([rows[c : c + 1] for c in range(3)], 1)


def routed_sum(chosen, first, rows, values):
    number = lax.broadcasted_iota(jnp.int32, (rows, chosen.shape[1]), 0) + first
    hot = jnp.where(number == chosen, 1.0, 0.0).astype(bf16)
    width = values.shape[1]
    parts = jnp.concatenate(split3(values), 1).astype(bf16)
    out = jnp.dot(hot, parts, preferred_element_type=f32)
    return out[:, :width] + out[:, width : 2 * width] + out[:, 2 * width :]


def step_kernel(
    domains, steps, send, pairs, send_row, pair_row, start, final, density,
    state, blocks, press, entropy, masses, own_m, pair_m, r_own, r_pair, f_own, f_pair, f_sum,
    p_out, p_in, r_out, r_in, q_out, q_in, f_out, f_in, send_sem, recv_sem,
):
    local = start.shape[0]
    total = local + 2 * GHOSTS
    dom = lax.axis_index("dom")
    has_low, has_high = dom > 0, dom < domains - 1
    row = lax.broadcasted_iota(jnp.int32, (8, 128), 0)

    def links(s, phase, out, into):
        def copy(side, target):
            return pltpu.make_async_remote_copy(
                src_ref=out.at[s, side],
                dst_ref=into.at[s, 1 - side],
                send_sem=send_sem.at[s, phase, side],
                recv_sem=recv_sem.at[s, phase, 1 - side],
                device_id={"dom": target},
                device_id_type=pl.DeviceIdType.MESH,
            )

        return copy(0, dom - 1), copy(1, dom + 1)

    def begin(s, phase, out, into):
        to_low, to_high = links(s, phase, out, into)
        pl.when(has_low)(to_low.start)
        pl.when(has_high)(to_high.start)

    def finish(s, phase, out, into):
        to_low, to_high = links(s, phase, out, into)

        @pl.when(has_low)
        def _():
            to_low.wait_send()
            to_high.wait_recv()

        @pl.when(has_high)
        def _():
            to_high.wait_send()
            to_low.wait_recv()

    if domains > 1:
        barrier = pltpu.get_barrier_semaphore()

        def greet(target):
            pl.semaphore_signal(
                barrier, inc=1, device_id={"dom": target}, device_id_type=pl.DeviceIdType.MESH
            )

        pl.when(has_low)(lambda: greet(dom - 1))
        pl.when(has_high)(lambda: greet(dom + 1))

    for side, has in ((0, has_low), (1, has_high)):

        @pl.when(jnp.logical_not(has))
        def _(side=side):
            for s in range(steps):
                p_in[s, side] = jnp.concatenate(
                    [jnp.zeros((GHOSTS, 3, 128), f32), jnp.full((GHOSTS, 1, 128), NONE, f32)], 1
                )
                for into in (r_in, q_in, f_in):
                    into[s, side] = jnp.zeros(into.shape[2:], f32)

    def enter(i):
        block = start[i]
        state[i] = block
        entropy[pl.ds(i, 1), :] = block[6:7]
        masses[pl.ds(i, 1), :] = block[7:8]

    each(local, enter)

    for s in range(steps):

        def scaled(i):
            block = state[i]
            level = jnp.log2(block[7:8])
            blocks[i] = jnp.concatenate(
                [block[0:3] * SCALE, level, level, jnp.zeros((3, 128), f32)], 0
            )

        each(local, scaled)

        def pick(j):
            for side in range(2):
                p_out[s, side, j] = blocks[send[s, side * GHOSTS + j]][0:4]

        each(GHOSTS, pick)
        if s == 0 and domains > 1:
            pl.semaphore_wait(barrier, has_low.astype(jnp.int32) + has_high.astype(jnp.int32))
        if domains > 1:
            begin(s, 0, p_out, p_in)

        def own_density(i):
            block = blocks[i]
            block = features(block, centre_of(block, row), row)
            m = weights_of(block, (block,), row)
            r_own[pl.ds(i, 1), :] = column_sum(m)
            h, l = split2(m)
            own_m[i, 0:128] = h
            own_m[i, 128:256] = l

        each(local, own_density, 32)
        if domains > 1:
            finish(s, 0, p_out, p_in)

        def ghost(j):
            for side in range(2):
                block = p_in[s, side, j]
                blocks[local + side * GHOSTS + j] = jnp.concatenate(
                    [block, block[3:4], jnp.zeros((3, 128), f32)], 0
                )

        each(GHOSTS, ghost)

        def pair_density(i):
            block = blocks[i]
            centre = centre_of(block, row)
            own, first, second = (
                features(b, centre, row)
                for b in (block, blocks[pairs[s, 2 * i]], blocks[pairs[s, 2 * i + 1]])
            )
            m = weights_of(own, (first, second), row)
            sums = column_sum(m)
            r_pair[pl.ds(2 * i, 1), :] = sums[:, :128]
            r_pair[pl.ds(2 * i + 1, 1), :] = sums[:, 128:]
            back = jnp.concatenate(split2(m[:, :128] + m[:, 128:]), 1)
            back = lax.dot_general(
                jnp.ones((8, 256), bf16), back, (((1,), (1,)), ((), ())), preferred_element_type=f32
            )
            r_own[pl.ds(i, 1), :] += back[0:1]
            h, l = split2(m)
            pair_m[i, :, 0:256] = h
            pair_m[i, :, 256:512] = l

        each(local, pair_density, 16)
        chosen = pair_row[s]
        sent = send_row[s]
        for side in range(2):
            r_out[s, side] = routed_sum(chosen, local + side * GHOSTS, GHOSTS, r_pair[...])
        for part in range(0, local, 128):
            r_own[part : part + 128] += routed_sum(chosen, part, 128, r_pair[...])
        if domains > 1:
            begin(s, 1, r_out, r_in)
            finish(s, 1, r_out, r_in)
        incoming = jnp.concatenate([r_in[s, 0], r_in[s, 1]], 0)
        rho = (r_own[...] + routed_sum(sent, 0, local, incoming)) / masses[...]
        if s == steps - 1:
            density[...] = rho
        press[0:local] = entropy[...] * jnp.exp2(jnp.log2(rho) * (-1.0 / 3.0))

        def pick_press(j):
            for side in range(2):
                q_out[s, side, pl.ds(j, 1), :] = press[pl.ds(send[s, side * GHOSTS + j], 1), :]

        each(GHOSTS, pick_press)
        if domains > 1:
            begin(s, 2, q_out, q_in)

        def own_force(i):
            block = blocks[i]
            v = vector_rows(block - centre_of(block, row), press[pl.ds(i, 1), :])
            vv = halves(v)
            y = join(
                jnp.dot(jnp.concatenate([vv, vv], 1), own_m[i], preferred_element_type=f32)
            )
            f_own[pl.ds(i, 1), :] = lanes(force_rows(v, y))

        each(local, own_force, 32)
        if domains > 1:
            finish(s, 2, q_out, q_in)
        press[local : local + GHOSTS] = q_in[s, 0]
        press[local + GHOSTS : total] = q_in[s, 1]

        def pair_force(i):
            block = blocks[i]
            centre = centre_of(block, row)
            n1, n2 = pairs[s, 2 * i], pairs[s, 2 * i + 1]
            vs = [
                vector_rows(b - centre, press[pl.ds(n, 1), :])
                for b, n in ((block, i), (blocks[n1], n1), (blocks[n2], n2))
            ]
            own, first, second = (halves(v) for v in vs)
            far = jnp.concatenate([first, second, first, second], 1)
            across = lax.dot_general(
                pair_m[i], far, (((1,), (1,)), ((), ())), preferred_element_type=f32
            ).T
            f_own[pl.ds(i, 1), :] += lanes(force_rows(vs[0], join(across)))
            stacked = jnp.concatenate([pair_m[i, :, 0:256], pair_m[i, :, 256:512]], 0)
            down = join(
                jnp.dot(jnp.concatenate([own, own], 1), stacked, preferred_element_type=f32)
            )
            f_pair[pl.ds(2 * i, 1), :] = lanes(force_rows(vs[1], down[:, :128]))
            f_pair[pl.ds(2 * i + 1, 1), :] = lanes(force_rows(vs[2], down[:, 128:]))

        each(local, pair_force, 32)
        for side in range(2):
            f_out[s, side] = routed_sum(chosen, local + side * GHOSTS, GHOSTS, f_pair[...])
        for part in range(0, local, 128):
            f_own[part : part + 128] += routed_sum(chosen, part, 128, f_pair[...])
        if domains > 1:
            begin(s, 3, f_out, f_in)
            finish(s, 3, f_out, f_in)
        incoming = jnp.concatenate([f_in[s, 0], f_in[s, 1]], 0)
        for part in range(0, local, 128):
            f_sum[part : part + 128] = f_own[part : part + 128] + routed_sum(sent, part, 128, incoming)

        def move(i):
            block = state[i]
            push = f_sum[pl.ds(i, 1), :] * (STEP / SCALE)
            push = jnp.concatenate([push[:, 0:128], push[:, 128:256], push[:, 256:384]], 0)
            velocity = block[3:6] + push / block[7:8]
            position = block[0:3] + STEP * velocity
            if s == steps - 1:
                for c in range(3):
                    final[c, pl.ds(i, 1), :] = position[c : c + 1]
                    final[3 + c, pl.ds(i, 1), :] = velocity[c : c + 1]
            else:
                state[i] = jnp.concatenate([position, velocity, block[6:8]], 0)

        each(local, move)


def run_steps(domains, send, pairs, start):
    steps = send.shape[0]
    local = start.shape[0]
    total = local + 2 * GHOSTS
    vmem, smem = (pl.BlockSpec(memory_space=m) for m in (pltpu.VMEM, pltpu.SMEM))
    buffers = []
    for shape in ((GHOSTS, 4, 128), (GHOSTS, 128), (GHOSTS, 128), (GHOSTS, 384)):
        buffers += [pltpu.VMEM((steps, 2) + shape, f32)] * 2
    return pl.pallas_call(
        functools.partial(step_kernel, domains, steps),
        name="steps",
        out_shape=[
            jax.ShapeDtypeStruct((6, local, 128), f32),
            jax.ShapeDtypeStruct((local, 128), f32),
        ],
        in_specs=[smem, smem, vmem, vmem, vmem],
        out_specs=[vmem, vmem],
        scratch_shapes=[
            pltpu.VMEM((local, 8, 128), f32),
            pltpu.VMEM((total, 8, 128), f32),
            pltpu.VMEM((total, 128), f32),
            pltpu.VMEM((local, 128), f32),
            pltpu.VMEM((local, 128), f32),
            pltpu.VMEM((local, 256, 128), bf16),
            pltpu.VMEM((local, 128, 512), bf16),
            pltpu.VMEM((local, 128), f32),
            pltpu.VMEM((2 * local, 128), f32),
            pltpu.VMEM((local, 384), f32),
            pltpu.VMEM((2 * local, 384), f32),
            pltpu.VMEM((local, 384), f32),
            *buffers,
            pltpu.SemaphoreType.DMA((steps, 4, 2)),
            pltpu.SemaphoreType.DMA((steps, 4, 2)),
        ],
        compiler_params=pltpu.CompilerParams(
            vmem_limit_bytes=67_000_000,
            **(dict(collective_id=1, has_side_effects=True) if domains > 1 else {}),
        ),
    )(send, pairs, send[:, None], pairs[:, None], start)


def migrate_kernel(
    devices, pack_index, place_index, pos_vel, entropy, masses, state, packed, outbox, inbox, send_sem, recv_sem
):
    subs = lax.axis_size("sub")
    me = lax.axis_index("dom") * subs + lax.axis_index("sub")

    def device(k):
        there = lax.rem(me + k, devices)
        return {"dom": there // subs, "sub": lax.rem(there, subs)}

    mesh_id = pl.DeviceIdType.MESH
    barrier = pltpu.get_barrier_semaphore()

    def greet(k, _):
        pl.semaphore_signal(barrier, inc=1, device_id=device(k), device_id_type=mesh_id)
        return 0

    lax.fori_loop(1, devices, greet, 0)
    local = packed.shape[0]

    def gather(g):
        rows = pl.ds(pl.multiple_of(g * 8, 8), 8)
        for c in range(6):
            packed[rows, c, :] = pos_vel[c, rows, :]
        packed[rows, 6, :] = entropy[rows, :]
        packed[rows, 7, :] = masses[rows, :]

    each(local // 8, gather, 4)

    def pack(k):
        for r in range(MOST):
            outbox[k, r] = packed[pack_index[k * MOST + r]]

    each(devices, pack)
    pl.semaphore_wait(barrier, devices - 1)

    def copy(source, target, k):
        return pltpu.make_async_remote_copy(
            src_ref=source, dst_ref=target, send_sem=send_sem, recv_sem=recv_sem,
            device_id=device(k), device_id_type=mesh_id,
        )

    def send(j, _):
        k = lax.rem(j * 45, devices)
        copy(outbox.at[k], inbox.at[k], k).start()
        return 0

    lax.fori_loop(1, devices, send, 0)
    half = local // 2

    def stay(j):
        state[j] = packed[place_index[j]]

    each(half, stay)
    everything = pl.ds(1, devices - 1)
    whole = copy(outbox.at[everything], inbox.at[everything], 1)
    whole.wait_send()
    whole.wait_recv()

    def come(j):
        slot = place_index[half + j]
        state[half + j] = inbox[slot // MOST, lax.rem(slot, MOST)]

    each(half, come)


def migrate(devices, pack_index, place_index, pos_vel, entropy, masses):
    local, size = entropy.shape
    vmem, smem = (pl.BlockSpec(memory_space=m) for m in (pltpu.VMEM, pltpu.SMEM))
    block = (local, 8, size)
    return pl.pallas_call(
        functools.partial(migrate_kernel, devices),
        name="migrate",
        out_shape=jax.ShapeDtypeStruct(block, f32),
        in_specs=[smem, smem, vmem, vmem, vmem],
        out_specs=vmem,
        scratch_shapes=[
            pltpu.VMEM(block, f32),
            pltpu.VMEM((devices, MOST, 8, size), f32),
            pltpu.VMEM((devices, MOST, 8, size), f32),
            pltpu.SemaphoreType.DMA,
            pltpu.SemaphoreType.DMA,
        ],
        compiler_params=pltpu.CompilerParams(collective_id=2, has_side_effects=True),
    )(pack_index, place_index, pos_vel, entropy, masses)


def shards(pos_vel, entropy, masses, destination, ghost_send, pair_list):
    devices = lax.axis_size(("dom", "sub"))
    me = lax.axis_index(("dom", "sub"))
    local = pos_vel.shape[0]
    number = jnp.arange(local, dtype=jnp.int32)
    device = jnp.arange(devices, dtype=jnp.int32)
    slot = jnp.arange(devices * MOST, dtype=jnp.int32)
    same = destination[:, None] == destination[None, :]
    rank = jnp.sum((same & (number[:, None] < number[None, :])).astype(jnp.int32), 0)
    staying = destination == me
    shift = (destination - me) % devices
    out_slot = jnp.where(staying, -1, shift * MOST + rank)
    pack_index = jnp.sum(jnp.where(out_slot[:, None] == slot[None, :], number[:, None], 0), 0)
    source = (me - device) % devices
    come = jnp.sum((shift[:, None] == device[None, :]).astype(jnp.int32), 0)
    come = jnp.where(device == 0, 0, come)
    before = jnp.sum(jnp.where(source[:, None] < source[None, :], come[:, None], 0), 0)
    half = local - devices
    stay_index = jnp.sum(
        jnp.where(staying[:, None] & (rank[:, None] == number[None, :half]), number[:, None], 0), 0
    )
    come_index = sum(
        jnp.sum(
            jnp.where((before[:, None] + r == device[None, :]) & (come[:, None] > r), device[:, None] * MOST + r, 0), 0
        )
        for r in range(MOST)
    )
    place_index = jnp.concatenate([stay_index, come_index])
    state = migrate(
        devices, pack_index, place_index, jnp.transpose(pos_vel, (1, 0, 2)), entropy, masses
    )
    steps = ghost_send.shape[0]
    final, density = run_steps(lax.axis_size("dom"), ghost_send, pair_list.reshape(steps, -1), state)
    return jnp.transpose(final, (1, 0, 2)), density


def solution(mesh):
    both = ("dom", "sub")
    in_specs = (P(both, None, None), P(both, None), P(both, None), P(both), P(None, both), P(None, both, None))
    out_specs = (P(both, None, None), P(both, None))
    return jax.shard_map(shards, mesh=mesh, in_specs=in_specs, out_specs=out_specs, check_vma=False)
```

```python
import functools
import math

import jax
import jax.numpy as jnp
from jax import lax
from jax.experimental import pallas as pl
from jax.experimental.pallas import tpu as pltpu
from jax.sharding import PartitionSpec as P

f32, bf16 = jnp.float32, jnp.bfloat16
SCALE = math.sqrt(math.log2(math.e))


def rounded(x):
    return x.astype(bf16).astype(f32)


def split3(x):
    high = rounded(x)
    rest = x - high
    mid = rounded(rest)
    return high, mid, rest - mid


def split2(x):
    high = x.astype(bf16)
    return high, (x - high.astype(f32)).astype(bf16)


def features(block, centre, row):
    moved = block - centre
    square = jnp.where(row < 3, moved * moved, 0.0)
    half = 0.5 * jnp.sum(square, axis=0, keepdims=True)
    return jnp.where((row == 3) | (row == 4), moved - half, moved)


def left_rows(moved, row):
    h, m, l = split3(jnp.where(row == 4, 1.0, moved))
    return jnp.concatenate([h, h, m, m, h, l], 0).astype(bf16)


def right_rows(moved, row):
    h, m, l = split3(jnp.where(row == 3, 1.0, moved))
    return jnp.concatenate([h, m, h, m, l, h], 0).astype(bf16)


def centre_of(block, row):
    return jnp.where(row < 3, jnp.mean(block, axis=1, keepdims=True), 0.0)


def weights_of(left, parts, row):
    right = jnp.concatenate([right_rows(p, row) for p in parts], 1)
    exponent = lax.dot_general(
        left_rows(left, row), right, (((0,), (0,)), ((), ())), preferred_element_type=f32
    )
    return jnp.exp2(exponent)


def fold(x):
    return jnp.sum(x.reshape(-1, 8, x.shape[-1]), 0)


MOST = 2
STEP = 0.25
UNROLL = 8
GHOSTS = 64
NONE = -300.0


def each(count, body, unroll=8):
    def group(g, _):
        for u in range(unroll):
            body(g * unroll + u)
        return 0

    lax.fori_loop(0, count // unroll, group, 0)


def column_sum(x):
    return jnp.sum(fold(x), axis=0, keepdims=True)


def force_rows(v, y):
    x, qx, q = v[0:3], v[3:6], v[6:7]
    return qx * y[7:8] + x * y[6:7] - q * y[0:3] - y[3:6]


def vector_rows(moved, q):
    x = moved[0:3]
    return jnp.concatenate([x, x * q, q, jnp.ones_like(q)], 0)


def halves(v):
    return jnp.concatenate(split2(v), 0)


def join(y):
    return y[0:8] + y[8:16]


def lanes(rows):
    return jnp.concatenate([rows[c : c + 1] for c in range(3)], 1)


def routed_sum(chosen, first, rows, values):
    number = lax.broadcasted_iota(jnp.int32, (rows, chosen.shape[1]), 0) + first
    hot = jnp.where(number == chosen, 1.0, 0.0).astype(bf16)
    width = values.shape[1]
    parts = jnp.concatenate(split3(values), 1).astype(bf16)
    out = jnp.dot(hot, parts, preferred_element_type=f32)
    return out[:, :width] + out[:, width : 2 * width] + out[:, 2 * width :]


def step_kernel(
    domains, subs, steps, pack_index, place_index, send, pairs, send_row, pair_row,
    pos_vel, entropy_in, masses_in, final, density, outbox, inbox, state, blocks, press, entropy, masses, own_m, pair_m, r_own, r_pair, f_own, f_pair, f_sum,
    p_out, p_in, r_out, r_in, q_out, q_in, f_out, f_in, send_sem, recv_sem, move_sems,
):
    local = state.shape[0]
    half = local // 2
    devices = domains * subs
    several = devices > 1
    total = local + 2 * GHOSTS
    dom = lax.axis_index("dom")
    has_low, has_high = dom > 0, dom < domains - 1
    row = lax.broadcasted_iota(jnp.int32, (8, 128), 0)

    def links(s, phase, out, into):
        def copy(side, target):
            return pltpu.make_async_remote_copy(
                src_ref=out.at[s, side],
                dst_ref=into.at[s, 1 - side],
                send_sem=send_sem.at[s, phase, side],
                recv_sem=recv_sem.at[s, phase, 1 - side],
                device_id={"dom": target},
                device_id_type=pl.DeviceIdType.MESH,
            )

        return copy(0, dom - 1), copy(1, dom + 1)

    def begin(s, phase, out, into):
        to_low, to_high = links(s, phase, out, into)
        pl.when(has_low)(to_low.start)
        pl.when(has_high)(to_high.start)

    def finish(s, phase, out, into):
        to_low, to_high = links(s, phase, out, into)

        @pl.when(has_low)
        def _():
            to_low.wait_send()
            to_high.wait_recv()

        @pl.when(has_high)
        def _():
            to_high.wait_send()
            to_low.wait_recv()

    me = dom * subs + lax.axis_index("sub")
    mesh_id = pl.DeviceIdType.MESH

    def device(k):
        there = lax.rem(me + k, devices)
        return {"dom": there // subs, "sub": lax.rem(there, subs)}

    if several:
        barrier = pltpu.get_barrier_semaphore()

        def greet(k, _):
            pl.semaphore_signal(barrier, inc=1, device_id=device(k), device_id_type=mesh_id)
            return 0

        lax.fori_loop(1, devices, greet, 0)

    packed = blocks

    def gather(g):
        rows = pl.ds(pl.multiple_of(g * 8, 8), 8)
        for c in range(6):
            packed[rows, c, :] = pos_vel[c, rows, :]
        packed[rows, 6, :] = entropy_in[rows, :]
        packed[rows, 7, :] = masses_in[rows, :]

    each(local // 8, gather, 4)

    def pack(k):
        for r in range(MOST):
            outbox[k, r] = packed[pack_index[k * MOST + r]]

    each(devices, pack)

    for side, has in ((0, has_low), (1, has_high)):

        @pl.when(jnp.logical_not(has))
        def _(side=side):
            for s in range(steps):
                p_in[s, side] = jnp.concatenate(
                    [jnp.zeros((GHOSTS, 3, 128), f32), jnp.full((GHOSTS, 1, 128), NONE, f32)], 1
                )
                for into in (r_in, q_in, f_in):
                    into[s, side] = jnp.zeros(into.shape[2:], f32)

    def copy(source, target, k):
        return pltpu.make_async_remote_copy(
            src_ref=source, dst_ref=target, send_sem=move_sems.at[0], recv_sem=move_sems.at[1],
            device_id=device(k), device_id_type=mesh_id,
        )

    if several:
        pl.semaphore_wait(barrier, devices - 1)

        def send_moving(j, _):
            k = lax.rem(j * 45, devices)
            copy(outbox.at[k], inbox.at[k], k).start()
            return 0

        lax.fori_loop(1, devices, send_moving, 0)

    def enter(i, block):
        state[i] = block
        entropy[pl.ds(i, 1), :] = block[6:7]
        masses[pl.ds(i, 1), :] = block[7:8]

    def scaled(i):
        block = state[i]
        level = jnp.log2(block[7:8])
        blocks[i] = jnp.concatenate(
            [block[0:3] * SCALE, level, level, jnp.zeros((3, 128), f32)], 0
        )

    def own_density(i):
        block = blocks[i]
        block = features(block, centre_of(block, row), row)
        m = weights_of(block, (block,), row)
        r_own[pl.ds(i, 1), :] = column_sum(m)
        h, l = split2(m)
        own_m[i, 0:128] = h
        own_m[i, 128:256] = l

    each(half, lambda j: enter(j, packed[place_index[j]]))
    each(half, scaled)
    each(half, own_density, 32)
    if several:
        everything = pl.ds(1, devices - 1)
        whole = copy(outbox.at[everything], inbox.at[everything], 1)
        whole.wait_send()
        whole.wait_recv()

    def come(j):
        slot = place_index[half + j]
        enter(half + j, inbox[slot // MOST, lax.rem(slot, MOST)])
        scaled(half + j)

    each(half, come)

    for s in range(steps):

        if s > 0:
            each(local, scaled)

        def pick(j):
            for side in range(2):
                p_out[s, side, j] = blocks[send[s, side * GHOSTS + j]][0:4]

        each(GHOSTS, pick)
        if domains > 1:
            begin(s, 0, p_out, p_in)

        if s == 0:
            each(local - half, lambda j: own_density(half + j), 32)
        else:
            each(local, own_density, 32)
        if domains > 1:
            finish(s, 0, p_out, p_in)

        def ghost(j):
            for side in range(2):
                block = p_in[s, side, j]
                blocks[local + side * GHOSTS + j] = jnp.concatenate(
                    [block, block[3:4], jnp.zeros((3, 128), f32)], 0
                )

        each(GHOSTS, ghost)

        def pair_density(i):
            block = blocks[i]
            centre = centre_of(block, row)
            own, first, second = (
                features(b, centre, row)
                for b in (block, blocks[pairs[s, 0, i]], blocks[pairs[s, 1, i]])
            )
            m = weights_of(own, (first, second), row)
            sums = column_sum(m)
            r_pair[pl.ds(i, 1), :] = sums[:, :128]
            r_pair[pl.ds(local + i, 1), :] = sums[:, 128:]
            back = jnp.concatenate(split2(m[:, :128] + m[:, 128:]), 1)
            back = lax.dot_general(
                jnp.ones((8, 256), bf16), back, (((1,), (1,)), ((), ())), preferred_element_type=f32
            )
            r_own[pl.ds(i, 1), :] += back[0:1]
            h, l = split2(m)
            pair_m[i, :, 0:256] = h
            pair_m[i, :, 256:512] = l

        each(local, pair_density, 32)
        chosen = jnp.concatenate([pair_row[s, 0:1], pair_row[s, 1:2]], 1)
        sent = send_row[s : s + 1, :]
        for side in range(2):
            r_out[s, side] = routed_sum(chosen, local + side * GHOSTS, GHOSTS, r_pair[...])
        for part in range(0, local, 128):
            r_own[part : part + 128] += routed_sum(chosen, part, 128, r_pair[...])
        if domains > 1:
            begin(s, 1, r_out, r_in)
            finish(s, 1, r_out, r_in)
        incoming = jnp.concatenate([r_in[s, 0], r_in[s, 1]], 0)
        rho = (r_own[...] + routed_sum(sent, 0, local, incoming)) / masses[...]
        if s == steps - 1:
            density[...] = rho
        press[0:local] = entropy[...] * jnp.exp2(jnp.log2(rho) * (-1.0 / 3.0))

        def pick_press(j):
            for side in range(2):
                q_out[s, side, pl.ds(j, 1), :] = press[pl.ds(send[s, side * GHOSTS + j], 1), :]

        each(GHOSTS, pick_press)
        if domains > 1:
            begin(s, 2, q_out, q_in)

        def own_force(i):
            block = blocks[i]
            v = vector_rows(block - centre_of(block, row), press[pl.ds(i, 1), :])
            vv = halves(v)
            y = join(
                jnp.dot(jnp.concatenate([vv, vv], 1), own_m[i], preferred_element_type=f32)
            )
            f_own[pl.ds(i, 1), :] = lanes(force_rows(v, y))

        each(local, own_force, 32)
        if domains > 1:
            finish(s, 2, q_out, q_in)
        press[local : local + GHOSTS] = q_in[s, 0]
        press[local + GHOSTS : total] = q_in[s, 1]

        def pair_force(i):
            block = blocks[i]
            centre = centre_of(block, row)
            n1, n2 = pairs[s, 0, i], pairs[s, 1, i]
            vs = [
                vector_rows(b - centre, press[pl.ds(n, 1), :])
                for b, n in ((block, i), (blocks[n1], n1), (blocks[n2], n2))
            ]
            own, first, second = (halves(v) for v in vs)
            far = jnp.concatenate([first, second, first, second], 1)
            across = lax.dot_general(
                pair_m[i], far, (((1,), (1,)), ((), ())), preferred_element_type=f32
            ).T
            f_own[pl.ds(i, 1), :] += lanes(force_rows(vs[0], join(across)))
            stacked = jnp.concatenate([pair_m[i, :, 0:256], pair_m[i, :, 256:512]], 0)
            down = join(
                jnp.dot(jnp.concatenate([own, own], 1), stacked, preferred_element_type=f32)
            )
            f_pair[pl.ds(i, 1), :] = lanes(force_rows(vs[1], down[:, :128]))
            f_pair[pl.ds(local + i, 1), :] = lanes(force_rows(vs[2], down[:, 128:]))

        each(local, pair_force, 32)
        for side in range(2):
            f_out[s, side] = routed_sum(chosen, local + side * GHOSTS, GHOSTS, f_pair[...])
        for part in range(0, local, 128):
            f_own[part : part + 128] += routed_sum(chosen, part, 128, f_pair[...])
        if domains > 1:
            begin(s, 3, f_out, f_in)
            finish(s, 3, f_out, f_in)
        incoming = jnp.concatenate([f_in[s, 0], f_in[s, 1]], 0)
        for part in range(0, local, 128):
            f_sum[part : part + 128] = f_own[part : part + 128] + routed_sum(sent, part, 128, incoming)

        def move(i):
            block = state[i]
            push = f_sum[pl.ds(i, 1), :] * (STEP / SCALE)
            push = jnp.concatenate([push[:, 0:128], push[:, 128:256], push[:, 256:384]], 0)
            velocity = block[3:6] + push / block[7:8]
            position = block[0:3] + STEP * velocity
            if s == steps - 1:
                for c in range(3):
                    final[c, pl.ds(i, 1), :] = position[c : c + 1]
                    final[3 + c, pl.ds(i, 1), :] = velocity[c : c + 1]
            else:
                state[i] = jnp.concatenate([position, velocity, block[6:8]], 0)

        each(local, move)


def run_steps(domains, subs, pack_index, place_index, send, pairs, pos_vel, entropy, masses):
    steps = send.shape[0]
    local = pos_vel.shape[1]
    devices = domains * subs
    total = local + 2 * GHOSTS
    vmem, smem = (pl.BlockSpec(memory_space=m) for m in (pltpu.VMEM, pltpu.SMEM))
    buffers = []
    for shape in ((GHOSTS, 4, 128), (GHOSTS, 128), (GHOSTS, 128), (GHOSTS, 384)):
        buffers += [pltpu.VMEM((steps, 2) + shape, f32)] * 2
    return pl.pallas_call(
        functools.partial(step_kernel, domains, subs, steps),
        name="steps",
        out_shape=[
            jax.ShapeDtypeStruct((6, local, 128), f32),
            jax.ShapeDtypeStruct((local, 128), f32),
        ],
        in_specs=[smem] * 4 + [vmem] * 5,
        out_specs=[vmem, vmem],
        scratch_shapes=[
            pltpu.VMEM((devices, MOST, 8, 128), f32),
            pltpu.VMEM((devices, MOST, 8, 128), f32),
            pltpu.VMEM((local, 8, 128), f32),
            pltpu.VMEM((total, 8, 128), f32),
            pltpu.VMEM((total, 128), f32),
            pltpu.VMEM((local, 128), f32),
            pltpu.VMEM((local, 128), f32),
            pltpu.VMEM((local, 256, 128), bf16),
            pltpu.VMEM((local, 128, 512), bf16),
            pltpu.VMEM((local, 128), f32),
            pltpu.VMEM((2 * local, 128), f32),
            pltpu.VMEM((local, 384), f32),
            pltpu.VMEM((2 * local, 384), f32),
            pltpu.VMEM((local, 384), f32),
            *buffers,
            pltpu.SemaphoreType.DMA((steps, 4, 2)),
            pltpu.SemaphoreType.DMA((steps, 4, 2)),
            pltpu.SemaphoreType.DMA((2,)),
        ],
        compiler_params=pltpu.CompilerParams(
            vmem_limit_bytes=67_000_000,
            **(dict(collective_id=1, has_side_effects=True) if devices > 1 else {}),
        ),
    )(pack_index, place_index, send, pairs, send, pairs, pos_vel, entropy, masses)


def shards(pos_vel, entropy, masses, destination, ghost_send, pair_list):
    devices = lax.axis_size(("dom", "sub"))
    me = lax.axis_index(("dom", "sub"))
    local = pos_vel.shape[0]
    number = jnp.arange(local, dtype=jnp.int32)
    device = jnp.arange(devices, dtype=jnp.int32)
    slot = jnp.arange(devices * MOST, dtype=jnp.int32)
    same = destination[:, None] == destination[None, :]
    rank = jnp.sum((same & (number[:, None] < number[None, :])).astype(jnp.int32), 0)
    staying = destination == me
    shift = (destination - me) % devices
    out_slot = jnp.where(staying, -1, shift * MOST + rank)
    pack_index = jnp.sum(jnp.where(out_slot[:, None] == slot[None, :], number[:, None], 0), 0)
    source = (me - device) % devices
    come = jnp.sum((shift[:, None] == device[None, :]).astype(jnp.int32), 0)
    come = jnp.where(device == 0, 0, come)
    before = jnp.sum(jnp.where(source[:, None] < source[None, :], come[:, None], 0), 0)
    half = local - devices
    stay_index = jnp.sum(
        jnp.where(staying[:, None] & (rank[:, None] == number[None, :half]), number[:, None], 0), 0
    )
    come_index = sum(
        jnp.sum(
            jnp.where((before[:, None] + r == device[None, :]) & (come[:, None] > r), device[:, None] * MOST + r, 0), 0
        )
        for r in range(MOST)
    )
    place_index = jnp.concatenate([stay_index, come_index])
    final, density = run_steps(
        lax.axis_size("dom"), lax.axis_size("sub"), pack_index, place_index, ghost_send,
        jnp.transpose(pair_list, (0, 2, 1)), jnp.transpose(pos_vel, (1, 0, 2)), entropy, masses,
    )
    return jnp.transpose(final, (1, 0, 2)), density


def solution(mesh):
    both = ("dom", "sub")
    in_specs = (P(both, None, None), P(both, None), P(both, None), P(both), P(None, both), P(None, both, None))
    out_specs = (P(both, None, None), P(both, None))
    return jax.shard_map(shards, mesh=mesh, in_specs=in_specs, out_specs=out_specs, check_vma=False)
```

```python
import functools
import math

import jax
import jax.numpy as jnp
from jax import lax
from jax.experimental import pallas as pl
from jax.experimental.pallas import tpu as pltpu
from jax.sharding import PartitionSpec as P

f32, bf16 = jnp.float32, jnp.bfloat16
SCALE = math.sqrt(math.log2(math.e))


def rounded(x):
    return x.astype(bf16).astype(f32)


def split3(x):
    high = rounded(x)
    rest = x - high
    mid = rounded(rest)
    return high, mid, rest - mid


def split2(x):
    high = x.astype(bf16)
    return high, (x - high.astype(f32)).astype(bf16)


def features(block, centre, row):
    moved = block - centre
    square = jnp.where(row < 3, moved * moved, 0.0)
    half = 0.5 * jnp.sum(square, axis=0, keepdims=True)
    return jnp.where((row == 3) | (row == 4), moved - half, moved)


def left_rows(moved, row):
    h, m, l = split3(jnp.where(row == 4, 1.0, moved))
    return jnp.concatenate([h, h, m, m, h, l], 0).astype(bf16)


def right_rows(moved, row):
    h, m, l = split3(jnp.where(row == 3, 1.0, moved))
    return jnp.concatenate([h, m, h, m, l, h], 0).astype(bf16)


def centre_of(block, row):
    return jnp.where(row < 3, jnp.mean(block, axis=1, keepdims=True), 0.0)


def weights_of(left, parts, row):
    right = jnp.concatenate([right_rows(p, row) for p in parts], 1)
    exponent = lax.dot_general(
        left_rows(left, row), right, (((0,), (0,)), ((), ())), preferred_element_type=f32
    )
    return jnp.exp2(exponent)


def fold(x):
    return jnp.sum(x.reshape(-1, 8, x.shape[-1]), 0)


MOST = 2
STEP = 0.25
UNROLL = 8
GHOSTS = 64
NONE = -300.0


def each(count, body, unroll=8):
    def group(g, _):
        for u in range(unroll):
            body(g * unroll + u)
        return 0

    lax.fori_loop(0, count // unroll, group, 0)


def column_sum(x):
    return jnp.sum(fold(x), axis=0, keepdims=True)


def force_rows(v, y):
    x, qx, q = v[0:3], v[3:6], v[6:7]
    return qx * y[7:8] + x * y[6:7] - q * y[0:3] - y[3:6]


def vector_rows(moved, q):
    x = moved[0:3]
    return jnp.concatenate([x, x * q, q, jnp.ones_like(q)], 0)


def halves(v):
    return jnp.concatenate(split2(v), 0)


def join(y):
    return y[0:8] + y[8:16]


def lanes(rows):
    return jnp.concatenate([rows[c : c + 1] for c in range(3)], 1)


def routed_sum(chosen, first, rows, values):
    number = lax.broadcasted_iota(jnp.int32, (rows, chosen.shape[1]), 0) + first
    hot = jnp.where(number == chosen, 1.0, 0.0).astype(bf16)
    width = values.shape[1]
    parts = jnp.concatenate(split3(values), 1).astype(bf16)
    out = jnp.dot(hot, parts, preferred_element_type=f32)
    return out[:, :width] + out[:, width : 2 * width] + out[:, 2 * width :]


def step_kernel(
    domains, subs, steps, pack_index, place_index, send, pairs, send_row, pair_row,
    pos_vel, entropy_in, masses_in, final, density, outbox, inbox, state, blocks, press, entropy, masses, own_m, pair_m, r_own, r_pair, f_own, f_pair, f_sum,
    p_out, p_in, r_out, r_in, q_out, q_in, f_out, f_in, send_sem, recv_sem, move_sems,
):
    local = state.shape[0]
    half = local // 2
    devices = domains * subs
    several = devices > 1
    total = local + 2 * GHOSTS
    dom = lax.axis_index("dom")
    has_low, has_high = dom > 0, dom < domains - 1
    row = lax.broadcasted_iota(jnp.int32, (8, 128), 0)

    def links(s, phase, out, into):
        def copy(side, target):
            return pltpu.make_async_remote_copy(
                src_ref=out.at[s, side],
                dst_ref=into.at[s, 1 - side],
                send_sem=send_sem.at[s, phase, side],
                recv_sem=recv_sem.at[s, phase, 1 - side],
                device_id={"dom": target},
                device_id_type=pl.DeviceIdType.MESH,
            )

        return copy(0, dom - 1), copy(1, dom + 1)

    def begin(s, phase, out, into):
        to_low, to_high = links(s, phase, out, into)
        pl.when(has_low)(to_low.start)
        pl.when(has_high)(to_high.start)

    def finish(s, phase, out, into):
        to_low, to_high = links(s, phase, out, into)

        @pl.when(has_low)
        def _():
            to_low.wait_send()
            to_high.wait_recv()

        @pl.when(has_high)
        def _():
            to_high.wait_send()
            to_low.wait_recv()

    me = dom * subs + lax.axis_index("sub")
    mesh_id = pl.DeviceIdType.MESH

    def device(k):
        there = lax.rem(me + k, devices)
        return {"dom": there // subs, "sub": lax.rem(there, subs)}

    if several:
        barrier = pltpu.get_barrier_semaphore()

        def greet(k, _):
            pl.semaphore_signal(barrier, inc=1, device_id=device(k), device_id_type=mesh_id)
            return 0

        lax.fori_loop(1, devices, greet, 0)

    packed = blocks

    def gather(g):
        rows = pl.ds(pl.multiple_of(g * 8, 8), 8)
        for c in range(6):
            packed[rows, c, :] = pos_vel[c, rows, :]
        packed[rows, 6, :] = entropy_in[rows, :]
        packed[rows, 7, :] = masses_in[rows, :]

    each(local // 8, gather, 4)

    def pack(k):
        for r in range(MOST):
            outbox[k, r] = packed[pack_index[k * MOST + r]]

    each(devices, pack)

    for side, has in ((0, has_low), (1, has_high)):

        @pl.when(jnp.logical_not(has))
        def _(side=side):
            for s in range(steps):
                p_in[s, side] = jnp.concatenate(
                    [jnp.zeros((GHOSTS, 3, 128), f32), jnp.full((GHOSTS, 1, 128), NONE, f32)], 1
                )
                for into in (r_in, q_in, f_in):
                    into[s, side] = jnp.zeros(into.shape[2:], f32)

    def copy(source, target, k):
        return pltpu.make_async_remote_copy(
            src_ref=source, dst_ref=target, send_sem=move_sems.at[0], recv_sem=move_sems.at[1],
            device_id=device(k), device_id_type=mesh_id,
        )

    if several:
        pl.semaphore_wait(barrier, devices - 1)

        def send_moving(j, _):
            k = lax.rem(j * 45, devices)
            copy(outbox.at[k], inbox.at[k], k).start()
            return 0

        lax.fori_loop(1, devices, send_moving, 0)

    def enter(i, block):
        state[i] = block
        entropy[pl.ds(i, 1), :] = block[6:7]
        masses[pl.ds(i, 1), :] = block[7:8]

    def scaled(i):
        block = state[i]
        level = jnp.log2(block[7:8])
        blocks[i] = jnp.concatenate(
            [block[0:3] * SCALE, level, level, jnp.zeros((3, 128), f32)], 0
        )

    def own_density(i):
        block = blocks[i]
        block = features(block, centre_of(block, row), row)
        m = weights_of(block, (block,), row)
        r_own[pl.ds(i, 1), :] = column_sum(m)
        h, l = split2(m)
        own_m[i, 0:128] = h
        own_m[i, 128:256] = l

    each(half, lambda j: enter(j, packed[place_index[j]]))
    each(half, scaled)
    each(half, own_density, 64)
    if several:
        everything = pl.ds(1, devices - 1)
        whole = copy(outbox.at[everything], inbox.at[everything], 1)
        whole.wait_send()
        whole.wait_recv()

    def come(j):
        slot = place_index[half + j]
        enter(half + j, inbox[slot // MOST, lax.rem(slot, MOST)])
        scaled(half + j)

    each(half, come)

    for s in range(steps):

        if s > 0:
            each(local, scaled)

        def pick(j):
            for side in range(2):
                p_out[s, side, j] = blocks[send[s, side * GHOSTS + j]][0:4]

        each(GHOSTS, pick)
        if domains > 1:
            begin(s, 0, p_out, p_in)

        if s == 0:
            each(local - half, lambda j: own_density(half + j), 64)
        else:
            each(local, own_density, 64)
        if domains > 1:
            finish(s, 0, p_out, p_in)

        def ghost(j):
            for side in range(2):
                block = p_in[s, side, j]
                blocks[local + side * GHOSTS + j] = jnp.concatenate(
                    [block, block[3:4], jnp.zeros((3, 128), f32)], 0
                )

        each(GHOSTS, ghost)

        def pair_density(i):
            block = blocks[i]
            centre = centre_of(block, row)
            own, first, second = (
                features(b, centre, row)
                for b in (block, blocks[pairs[s, 0, i]], blocks[pairs[s, 1, i]])
            )
            m = weights_of(own, (first, second), row)
            sums = column_sum(m)
            r_pair[pl.ds(i, 1), :] = sums[:, :128]
            r_pair[pl.ds(local + i, 1), :] = sums[:, 128:]
            back = jnp.concatenate(split2(m[:, :128] + m[:, 128:]), 1)
            back = lax.dot_general(
                jnp.ones((8, 256), bf16), back, (((1,), (1,)), ((), ())), preferred_element_type=f32
            )
            r_own[pl.ds(i, 1), :] += back[0:1]
            h, l = split2(m)
            pair_m[i, :, 0:256] = h
            pair_m[i, :, 256:512] = l

        each(local, pair_density, 64)
        chosen = jnp.concatenate([pair_row[s, 0:1], pair_row[s, 1:2]], 1)
        sent = send_row[s : s + 1, :]
        for side in range(2):
            r_out[s, side] = routed_sum(chosen, local + side * GHOSTS, GHOSTS, r_pair[...])
        for part in range(0, local, 128):
            r_own[part : part + 128] += routed_sum(chosen, part, 128, r_pair[...])
            if part == 0 and domains > 1:
                begin(s, 1, r_out, r_in)
        if domains > 1:
            finish(s, 1, r_out, r_in)
        incoming = jnp.concatenate([r_in[s, 0], r_in[s, 1]], 0)
        rho = (r_own[...] + routed_sum(sent, 0, local, incoming)) / masses[...]
        if s == steps - 1:
            density[...] = rho
        press[0:local] = entropy[...] * jnp.exp2(jnp.log2(rho) * (-1.0 / 3.0))

        def pick_press(j):
            for side in range(2):
                q_out[s, side, pl.ds(j, 1), :] = press[pl.ds(send[s, side * GHOSTS + j], 1), :]

        each(GHOSTS, pick_press)
        if domains > 1:
            begin(s, 2, q_out, q_in)

        def own_force(i):
            block = blocks[i]
            v = vector_rows(block - centre_of(block, row), press[pl.ds(i, 1), :])
            vv = halves(v)
            y = join(
                jnp.dot(jnp.concatenate([vv, vv], 1), own_m[i], preferred_element_type=f32)
            )
            f_own[pl.ds(i, 1), :] = lanes(force_rows(v, y))

        each(local, own_force, 64)
        if domains > 1:
            finish(s, 2, q_out, q_in)
        press[local : local + GHOSTS] = q_in[s, 0]
        press[local + GHOSTS : total] = q_in[s, 1]

        def pair_force(i):
            block = blocks[i]
            centre = centre_of(block, row)
            n1, n2 = pairs[s, 0, i], pairs[s, 1, i]
            vs = [
                vector_rows(b - centre, press[pl.ds(n, 1), :])
                for b, n in ((block, i), (blocks[n1], n1), (blocks[n2], n2))
            ]
            own, first, second = (halves(v) for v in vs)
            far = jnp.concatenate([first, second, first, second], 1)
            across = lax.dot_general(
                pair_m[i], far, (((1,), (1,)), ((), ())), preferred_element_type=f32
            ).T
            f_own[pl.ds(i, 1), :] += lanes(force_rows(vs[0], join(across)))
            stacked = jnp.concatenate([pair_m[i, :, 0:256], pair_m[i, :, 256:512]], 0)
            down = join(
                jnp.dot(jnp.concatenate([own, own], 1), stacked, preferred_element_type=f32)
            )
            f_pair[pl.ds(i, 1), :] = lanes(force_rows(vs[1], down[:, :128]))
            f_pair[pl.ds(local + i, 1), :] = lanes(force_rows(vs[2], down[:, 128:]))

        each(local, pair_force, 64)
        for side in range(2):
            f_out[s, side] = routed_sum(chosen, local + side * GHOSTS, GHOSTS, f_pair[...])
        for part in range(0, local, 128):
            f_own[part : part + 128] += routed_sum(chosen, part, 128, f_pair[...])
            if part == 0 and domains > 1:
                begin(s, 3, f_out, f_in)
        if domains > 1:
            finish(s, 3, f_out, f_in)
        incoming = jnp.concatenate([f_in[s, 0], f_in[s, 1]], 0)
        for part in range(0, local, 128):
            f_sum[part : part + 128] = f_own[part : part + 128] + routed_sum(sent, part, 128, incoming)

        def move(i):
            block = state[i]
            push = f_sum[pl.ds(i, 1), :] * (STEP / SCALE)
            push = jnp.concatenate([push[:, 0:128], push[:, 128:256], push[:, 256:384]], 0)
            velocity = block[3:6] + push / block[7:8]
            position = block[0:3] + STEP * velocity
            if s == steps - 1:
                for c in range(3):
                    final[c, pl.ds(i, 1), :] = position[c : c + 1]
                    final[3 + c, pl.ds(i, 1), :] = velocity[c : c + 1]
            else:
                state[i] = jnp.concatenate([position, velocity, block[6:8]], 0)

        each(local, move)


def run_steps(domains, subs, pack_index, place_index, send, pairs, pos_vel, entropy, masses):
    steps = send.shape[0]
    local = pos_vel.shape[1]
    devices = domains * subs
    total = local + 2 * GHOSTS
    vmem, smem = (pl.BlockSpec(memory_space=m) for m in (pltpu.VMEM, pltpu.SMEM))
    buffers = []
    for shape in ((GHOSTS, 4, 128), (GHOSTS, 128), (GHOSTS, 128), (GHOSTS, 384)):
        buffers += [pltpu.VMEM((steps, 2) + shape, f32)] * 2
    return pl.pallas_call(
        functools.partial(step_kernel, domains, subs, steps),
        name="steps",
        out_shape=[
            jax.ShapeDtypeStruct((6, local, 128), f32),
            jax.ShapeDtypeStruct((local, 128), f32),
        ],
        in_specs=[smem] * 4 + [vmem] * 5,
        out_specs=[vmem, vmem],
        scratch_shapes=[
            pltpu.VMEM((devices, MOST, 8, 128), f32),
            pltpu.VMEM((devices, MOST, 8, 128), f32),
            pltpu.VMEM((local, 8, 128), f32),
            pltpu.VMEM((total, 8, 128), f32),
            pltpu.VMEM((total, 128), f32),
            pltpu.VMEM((local, 128), f32),
            pltpu.VMEM((local, 128), f32),
            pltpu.VMEM((local, 256, 128), bf16),
            pltpu.VMEM((local, 128, 512), bf16),
            pltpu.VMEM((local, 128), f32),
            pltpu.VMEM((2 * local, 128), f32),
            pltpu.VMEM((local, 384), f32),
            pltpu.VMEM((2 * local, 384), f32),
            pltpu.VMEM((local, 384), f32),
            *buffers,
            pltpu.SemaphoreType.DMA((steps, 4, 2)),
            pltpu.SemaphoreType.DMA((steps, 4, 2)),
            pltpu.SemaphoreType.DMA((2,)),
        ],
        compiler_params=pltpu.CompilerParams(
            vmem_limit_bytes=67_000_000,
            **(dict(collective_id=1, has_side_effects=True) if devices > 1 else {}),
        ),
    )(pack_index, place_index, send, pairs, send, pairs, pos_vel, entropy, masses)


def shards(pos_vel, entropy, masses, destination, ghost_send, pair_list):
    devices = lax.axis_size(("dom", "sub"))
    me = lax.axis_index(("dom", "sub"))
    local = pos_vel.shape[0]
    number = jnp.arange(local, dtype=jnp.int32)
    device = jnp.arange(devices, dtype=jnp.int32)
    slot = jnp.arange(devices * MOST, dtype=jnp.int32)
    same = destination[:, None] == destination[None, :]
    rank = jnp.sum((same & (number[:, None] < number[None, :])).astype(jnp.int32), 0)
    staying = destination == me
    shift = (destination - me) % devices
    out_slot = jnp.where(staying, -1, shift * MOST + rank)
    pack_index = jnp.sum(jnp.where(out_slot[:, None] == slot[None, :], number[:, None], 0), 0)
    source = (me - device) % devices
    come = jnp.sum((shift[:, None] == device[None, :]).astype(jnp.int32), 0)
    come = jnp.where(device == 0, 0, come)
    before = jnp.sum(jnp.where(source[:, None] < source[None, :], come[:, None], 0), 0)
    half = local - devices
    stay_index = jnp.sum(
        jnp.where(staying[:, None] & (rank[:, None] == number[None, :half]), number[:, None], 0), 0
    )
    come_index = sum(
        jnp.sum(
            jnp.where((before[:, None] + r == device[None, :]) & (come[:, None] > r), device[:, None] * MOST + r, 0), 0
        )
        for r in range(MOST)
    )
    place_index = jnp.concatenate([stay_index, come_index])
    final, density = run_steps(
        lax.axis_size("dom"), lax.axis_size("sub"), pack_index, place_index, ghost_send,
        jnp.transpose(pair_list, (0, 2, 1)), jnp.transpose(pos_vel, (1, 0, 2)), entropy, masses,
    )
    return jnp.transpose(final, (1, 0, 2)), density


def solution(mesh):
    both = ("dom", "sub")
    in_specs = (P(both, None, None), P(both, None), P(both, None), P(both), P(None, both), P(None, both, None))
    out_specs = (P(both, None, None), P(both, None))
    return jax.shard_map(shards, mesh=mesh, in_specs=in_specs, out_specs=out_specs, check_vma=False)
```

```python
import functools
import math

import jax
import jax.numpy as jnp
from jax import lax
from jax.experimental import pallas as pl
from jax.experimental.pallas import tpu as pltpu
from jax.sharding import PartitionSpec as P

f32, bf16 = jnp.float32, jnp.bfloat16
SCALE = math.sqrt(math.log2(math.e))


def rounded(x):
    return x.astype(bf16).astype(f32)


def split3(x):
    high = rounded(x)
    rest = x - high
    mid = rounded(rest)
    return high, mid, rest - mid


def split2(x):
    high = x.astype(bf16)
    return high, (x - high.astype(f32)).astype(bf16)


def features(block, centre, row):
    moved = block - centre
    square = jnp.where(row < 3, moved * moved, 0.0)
    half = 0.5 * jnp.sum(square, axis=0, keepdims=True)
    return jnp.where((row == 3) | (row == 4), moved - half, moved)


def left_rows(moved, row):
    h, m, l = split3(jnp.where(row == 4, 1.0, moved))
    return jnp.concatenate([h, h, m, m, h, l], 0).astype(bf16)


def right_rows(moved, row):
    h, m, l = split3(jnp.where(row == 3, 1.0, moved))
    return jnp.concatenate([h, m, h, m, l, h], 0).astype(bf16)


def centre_of(block, row):
    return jnp.where(row < 3, jnp.mean(block, axis=1, keepdims=True), 0.0)


def weights_of(left, parts, row):
    right = jnp.concatenate([right_rows(p, row) for p in parts], 1)
    exponent = lax.dot_general(
        left_rows(left, row), right, (((0,), (0,)), ((), ())), preferred_element_type=f32
    )
    return jnp.exp2(exponent)


def fold(x):
    return jnp.sum(x.reshape(-1, 8, x.shape[-1]), 0)


MOST = 2
STEP = 0.25
UNROLL = 8
GHOSTS = 64
NONE = -300.0


def each(count, body, unroll=8):
    def group(g, _):
        for u in range(unroll):
            body(g * unroll + u)
        return 0

    lax.fori_loop(0, count // unroll, group, 0)


def column_sum(x):
    return jnp.sum(fold(x), axis=0, keepdims=True)


def force_rows(v, y):
    x, qx, q = v[0:3], v[3:6], v[6:7]
    return qx * y[7:8] + x * y[6:7] - q * y[0:3] - y[3:6]


def vector_rows(moved, q):
    x = moved[0:3]
    return jnp.concatenate([x, x * q, q, jnp.ones_like(q)], 0)


def halves(v):
    return jnp.concatenate(split2(v), 0)


def join(y):
    return y[0:8] + y[8:16]


def lanes(rows):
    return jnp.concatenate([rows[c : c + 1] for c in range(3)], 1)


def routed_sum(chosen, first, rows, values):
    number = lax.broadcasted_iota(jnp.int32, (rows, chosen.shape[1]), 0) + first
    hot = jnp.where(number == chosen, 1.0, 0.0).astype(bf16)
    width = values.shape[1]
    parts = jnp.concatenate(split3(values), 1).astype(bf16)
    out = jnp.dot(hot, parts, preferred_element_type=f32)
    return out[:, :width] + out[:, width : 2 * width] + out[:, 2 * width :]


def slot_numbers(me, devices, chosen):
    local = chosen.shape[1]

    def down(x):
        return jnp.broadcast_to(x, (128, x.shape[1])).T

    def count(hit, value):
        return jnp.sum(jnp.where(hit, value, 0), axis=0, keepdims=True)

    def number(shape, axis):
        return lax.broadcasted_iota(jnp.int32, shape, axis)

    wide, tall, square = (local, local), (local, 128), (128, 128)
    column = down(chosen)
    same = jnp.concatenate([column] * (local // 128), 1) == chosen
    rank = count(same & (number(wide, 0) < number(wide, 1)), 1)
    stays = chosen == me
    shift = lax.rem(chosen - me + devices, devices)
    slot = jnp.where(stays, devices * MOST + rank, shift * MOST + rank)
    slot_down, shift_down = down(slot), down(jnp.where(stays, 0, shift))
    block, lane = number(tall, 0), number(tall, 1)
    rows = [
        count(slot_down == lane + first, block)
        for first in range(0, devices * MOST + local - devices, 128)
    ]
    come = count((shift_down == lane) & (lane > 0), 1)
    k, other = number(square, 1), number(square, 0)
    source, other_source = (lax.rem(me - x + devices, devices) for x in (k, other))
    before = count(other_source < source, down(come))
    arrive = 0
    for r in range(MOST):
        place = down(jnp.where(come > r, before + r, -1))
        arrive = arrive + count(place == k, other * MOST + r)
    return rows + [arrive]


def step_kernel(
    domains, subs, steps, send, pairs, chosen_device, send_row, pair_row,
    pos_vel, entropy_in, masses_in, final, density, outbox, inbox, state, blocks, press, entropy, masses, own_m, pair_m, r_own, r_pair, f_own, f_pair, f_sum,
    p_out, p_in, r_out, r_in, q_out, q_in, f_out, f_in, send_sem, recv_sem, move_sems, rows_out, index,
):
    local = state.shape[0]
    half = local // 2
    devices = domains * subs
    several = devices > 1
    total = local + 2 * GHOSTS
    dom = lax.axis_index("dom")
    has_low, has_high = dom > 0, dom < domains - 1
    row = lax.broadcasted_iota(jnp.int32, (8, 128), 0)

    def links(s, phase, out, into):
        def copy(side, target):
            return pltpu.make_async_remote_copy(
                src_ref=out.at[s, side],
                dst_ref=into.at[s, 1 - side],
                send_sem=send_sem.at[s, phase, side],
                recv_sem=recv_sem.at[s, phase, 1 - side],
                device_id={"dom": target},
                device_id_type=pl.DeviceIdType.MESH,
            )

        return copy(0, dom - 1), copy(1, dom + 1)

    def begin(s, phase, out, into):
        to_low, to_high = links(s, phase, out, into)
        pl.when(has_low)(to_low.start)
        pl.when(has_high)(to_high.start)

    def finish(s, phase, out, into):
        to_low, to_high = links(s, phase, out, into)

        @pl.when(has_low)
        def _():
            to_low.wait_send()
            to_high.wait_recv()

        @pl.when(has_high)
        def _():
            to_high.wait_send()
            to_low.wait_recv()

    me = dom * subs + lax.axis_index("sub")
    mesh_id = pl.DeviceIdType.MESH

    def device(k):
        there = lax.rem(me + k, devices)
        return {"dom": there // subs, "sub": lax.rem(there, subs)}

    if several:
        barrier = pltpu.get_barrier_semaphore()

        def greet(k, _):
            pl.semaphore_signal(barrier, inc=1, device_id=device(k), device_id_type=mesh_id)
            return 0

        lax.fori_loop(1, devices, greet, 0)

    for r, numbers in enumerate(slot_numbers(me, 128, chosen_device[...])):
        rows_out[r : r + 1] = numbers

    packed = blocks

    def gather(g):
        rows = pl.ds(pl.multiple_of(g * 8, 8), 8)
        for c in range(6):
            packed[rows, c, :] = pos_vel[c, rows, :]
        packed[rows, 6, :] = entropy_in[rows, :]
        packed[rows, 7, :] = masses_in[rows, :]

    each(local // 8, gather, 4)

    to_scalars = pltpu.make_async_copy(rows_out, index, move_sems.at[2])
    to_scalars.start()
    to_scalars.wait()
    slots = 128 * MOST

    def number(t):
        return index[t // 128, lax.rem(t, 128)]

    def pack(k):
        for r in range(MOST):
            outbox[k, r] = packed[number(k * MOST + r)]

    each(devices, pack)

    for side, has in ((0, has_low), (1, has_high)):

        @pl.when(jnp.logical_not(has))
        def _(side=side):
            for s in range(steps):
                p_in[s, side] = jnp.concatenate(
                    [jnp.zeros((GHOSTS, 3, 128), f32), jnp.full((GHOSTS, 1, 128), NONE, f32)], 1
                )
                for into in (r_in, q_in, f_in):
                    into[s, side] = jnp.zeros(into.shape[2:], f32)

    def copy(source, target, k):
        return pltpu.make_async_remote_copy(
            src_ref=source, dst_ref=target, send_sem=move_sems.at[0], recv_sem=move_sems.at[1],
            device_id=device(k), device_id_type=mesh_id,
        )

    if several:
        pl.semaphore_wait(barrier, devices - 1)

        def send_moving(j, _):
            k = lax.rem(j * 45, devices)
            copy(outbox.at[k], inbox.at[k], k).start()
            return 0

        lax.fori_loop(1, devices, send_moving, 0)

    def enter(i, block):
        state[i] = block
        entropy[pl.ds(i, 1), :] = block[6:7]
        masses[pl.ds(i, 1), :] = block[7:8]

    def scaled(g):
        rows = pl.ds(pl.multiple_of(g * 8, 8), 8)
        level = jnp.log2(masses[rows, :])
        for c in range(3):
            blocks[rows, c, :] = state[rows, c, :] * SCALE
            blocks[rows, 5 + c, :] = jnp.zeros((8, 128), f32)
        blocks[rows, 3, :] = level
        blocks[rows, 4, :] = level

    def own_density(i):
        block = blocks[i]
        block = features(block, centre_of(block, row), row)
        m = weights_of(block, (block,), row)
        r_own[pl.ds(i, 1), :] = column_sum(m)
        h, l = split2(m)
        own_m[i, 0:128] = h
        own_m[i, 128:256] = l

    each(half, lambda j: enter(j, packed[number(slots + j)]))
    each(half // 8, scaled, 4)
    each(half, own_density, 64)
    if several:
        everything = pl.ds(1, devices - 1)
        whole = copy(outbox.at[everything], inbox.at[everything], 1)
        whole.wait_send()
        whole.wait_recv()

    def come(j):
        slot = number(slots + half + j)
        enter(half + j, inbox[slot // MOST, lax.rem(slot, MOST)])

    each(half, come)
    each(half // 8, lambda g: scaled(half // 8 + g), 4)

    for s in range(steps):

        if s > 0:
            each(local // 8, scaled, 4)

        def pick(j):
            for side in range(2):
                p_out[s, side, j] = blocks[send[s, side * GHOSTS + j]][0:4]

        each(GHOSTS, pick)
        if domains > 1:
            begin(s, 0, p_out, p_in)

        if s == 0:
            each(local - half, lambda j: own_density(half + j), 64)
        else:
            each(local, own_density, 64)
        if domains > 1:
            finish(s, 0, p_out, p_in)

        def ghost(j):
            for side in range(2):
                block = p_in[s, side, j]
                blocks[local + side * GHOSTS + j] = jnp.concatenate(
                    [block, block[3:4], jnp.zeros((3, 128), f32)], 0
                )

        each(GHOSTS, ghost)

        def pair_density(i):
            block = blocks[i]
            centre = centre_of(block, row)
            own, first, second = (
                features(b, centre, row)
                for b in (block, blocks[pairs[s, 0, i]], blocks[pairs[s, 1, i]])
            )
            m = weights_of(own, (first, second), row)
            sums = column_sum(m)
            r_pair[pl.ds(i, 1), :] = sums[:, :128]
            r_pair[pl.ds(local + i, 1), :] = sums[:, 128:]
            back = jnp.concatenate(split2(m[:, :128] + m[:, 128:]), 1)
            back = lax.dot_general(
                jnp.ones((8, 256), bf16), back, (((1,), (1,)), ((), ())), preferred_element_type=f32
            )
            r_own[pl.ds(i, 1), :] += back[0:1]
            h, l = split2(m)
            pair_m[i, :, 0:256] = h
            pair_m[i, :, 256:512] = l

        each(local, pair_density, 64)
        chosen = jnp.concatenate([pair_row[s, 0:1], pair_row[s, 1:2]], 1)
        sent = send_row[s : s + 1, :]
        for side in range(2):
            r_out[s, side] = routed_sum(chosen, local + side * GHOSTS, GHOSTS, r_pair[...])
        for part in range(0, local, 128):
            r_own[part : part + 128] += routed_sum(chosen, part, 128, r_pair[...])
            if part == 0 and domains > 1:
                begin(s, 1, r_out, r_in)
        if domains > 1:
            finish(s, 1, r_out, r_in)
        incoming = jnp.concatenate([r_in[s, 0], r_in[s, 1]], 0)
        rho = (r_own[...] + routed_sum(sent, 0, local, incoming)) / masses[...]
        if s == steps - 1:
            density[...] = rho
        press[0:local] = entropy[...] * jnp.exp2(jnp.log2(rho) * (-1.0 / 3.0))

        def pick_press(j):
            for side in range(2):
                q_out[s, side, pl.ds(j, 1), :] = press[pl.ds(send[s, side * GHOSTS + j], 1), :]

        each(GHOSTS, pick_press)
        if domains > 1:
            begin(s, 2, q_out, q_in)

        def own_force(i):
            block = blocks[i]
            v = vector_rows(block - centre_of(block, row), press[pl.ds(i, 1), :])
            vv = halves(v)
            y = join(
                jnp.dot(jnp.concatenate([vv, vv], 1), own_m[i], preferred_element_type=f32)
            )
            f_own[pl.ds(i, 1), :] = lanes(force_rows(v, y))

        each(local, own_force, 64)
        if domains > 1:
            finish(s, 2, q_out, q_in)
        press[local : local + GHOSTS] = q_in[s, 0]
        press[local + GHOSTS : total] = q_in[s, 1]

        def pair_force(i):
            block = blocks[i]
            centre = centre_of(block, row)
            n1, n2 = pairs[s, 0, i], pairs[s, 1, i]
            vs = [
                vector_rows(b - centre, press[pl.ds(n, 1), :])
                for b, n in ((block, i), (blocks[n1], n1), (blocks[n2], n2))
            ]
            own, first, second = (halves(v) for v in vs)
            far = jnp.concatenate([first, second, first, second], 1)
            across = lax.dot_general(
                pair_m[i], far, (((1,), (1,)), ((), ())), preferred_element_type=f32
            ).T
            f_own[pl.ds(i, 1), :] += lanes(force_rows(vs[0], join(across)))
            stacked = jnp.concatenate([pair_m[i, :, 0:256], pair_m[i, :, 256:512]], 0)
            down = join(
                jnp.dot(jnp.concatenate([own, own], 1), stacked, preferred_element_type=f32)
            )
            f_pair[pl.ds(i, 1), :] = lanes(force_rows(vs[1], down[:, :128]))
            f_pair[pl.ds(local + i, 1), :] = lanes(force_rows(vs[2], down[:, 128:]))

        each(local, pair_force, 64)
        for side in range(2):
            f_out[s, side] = routed_sum(chosen, local + side * GHOSTS, GHOSTS, f_pair[...])
        for part in range(0, local, 128):
            f_own[part : part + 128] += routed_sum(chosen, part, 128, f_pair[...])
            if part == 0 and domains > 1:
                begin(s, 3, f_out, f_in)
        if domains > 1:
            finish(s, 3, f_out, f_in)
        incoming = jnp.concatenate([f_in[s, 0], f_in[s, 1]], 0)
        for part in range(0, local, 128):
            f_sum[part : part + 128] = f_own[part : part + 128] + routed_sum(sent, part, 128, incoming)

        def move(g):
            rows = pl.ds(pl.multiple_of(g * 8, 8), 8)
            gain = (STEP / SCALE) / masses[rows, :]
            for c in range(3):
                velocity = state[rows, 3 + c, :] + f_sum[rows, c * 128 : c * 128 + 128] * gain
                position = state[rows, c, :] + STEP * velocity
                if s == steps - 1:
                    final[c, rows, :] = position
                    final[3 + c, rows, :] = velocity
                else:
                    state[rows, c, :] = position
                    state[rows, 3 + c, :] = velocity

        each(local // 8, move, 4)


def run_steps(domains, subs, chosen, send, pairs, pos_vel, entropy, masses):
    steps = send.shape[0]
    local = pos_vel.shape[1]
    devices = domains * subs
    total = local + 2 * GHOSTS
    vmem, smem = (pl.BlockSpec(memory_space=m) for m in (pltpu.VMEM, pltpu.SMEM))
    buffers = []
    for shape in ((GHOSTS, 4, 128), (GHOSTS, 128), (GHOSTS, 128), (GHOSTS, 384)):
        buffers += [pltpu.VMEM((steps, 2) + shape, f32)] * 2
    return pl.pallas_call(
        functools.partial(step_kernel, domains, subs, steps),
        name="steps",
        out_shape=[
            jax.ShapeDtypeStruct((6, local, 128), f32),
            jax.ShapeDtypeStruct((local, 128), f32),
        ],
        in_specs=[smem] * 2 + [vmem] * 6,
        out_specs=[vmem, vmem],
        scratch_shapes=[
            pltpu.VMEM((devices, MOST, 8, 128), f32),
            pltpu.VMEM((devices, MOST, 8, 128), f32),
            pltpu.VMEM((local, 8, 128), f32),
            pltpu.VMEM((total, 8, 128), f32),
            pltpu.VMEM((total, 128), f32),
            pltpu.VMEM((local, 128), f32),
            pltpu.VMEM((local, 128), f32),
            pltpu.VMEM((local, 256, 128), bf16),
            pltpu.VMEM((local, 128, 512), bf16),
            pltpu.VMEM((local, 128), f32),
            pltpu.VMEM((2 * local, 128), f32),
            pltpu.VMEM((local, 384), f32),
            pltpu.VMEM((2 * local, 384), f32),
            pltpu.VMEM((local, 384), f32),
            *buffers,
            pltpu.SemaphoreType.DMA((steps, 4, 2)),
            pltpu.SemaphoreType.DMA((steps, 4, 2)),
            pltpu.SemaphoreType.DMA((3,)),
            pltpu.VMEM((4, 128), jnp.int32),
            pltpu.SMEM((4, 128), jnp.int32),
        ],
        compiler_params=pltpu.CompilerParams(
            vmem_limit_bytes=67_000_000,
            **(dict(collective_id=1, has_side_effects=True) if devices > 1 else {}),
        ),
    )(send, pairs, chosen, send, pairs, pos_vel, entropy, masses)


def shards(pos_vel, entropy, masses, destination, ghost_send, pair_list):
    final, density = run_steps(
        lax.axis_size("dom"), lax.axis_size("sub"), destination[None, :], ghost_send,
        jnp.transpose(pair_list, (0, 2, 1)), jnp.transpose(pos_vel, (1, 0, 2)), entropy, masses,
    )
    return jnp.transpose(final, (1, 0, 2)), density


def solution(mesh):
    both = ("dom", "sub")
    in_specs = (P(both, None, None), P(both, None), P(both, None), P(both), P(None, both), P(None, both, None))
    out_specs = (P(both, None, None), P(both, None))
    return jax.shard_map(shards, mesh=mesh, in_specs=in_specs, out_specs=out_specs, check_vma=False)
```

```python
import functools
import math

import jax
import jax.numpy as jnp
from jax import lax
from jax.experimental import pallas as pl
from jax.experimental.pallas import tpu as pltpu
from jax.sharding import PartitionSpec as P

f32, bf16 = jnp.float32, jnp.bfloat16
SCALE = math.sqrt(math.log2(math.e))


def rounded(x):
    return x.astype(bf16).astype(f32)


def split3(x):
    high = rounded(x)
    rest = x - high
    mid = rounded(rest)
    return high, mid, rest - mid


def split2(x):
    high = x.astype(bf16)
    return high, (x - high.astype(f32)).astype(bf16)


def features(block, centre, row):
    moved = block - centre
    square = jnp.where(row < 3, moved * moved, 0.0)
    half = 0.5 * jnp.sum(square, axis=0, keepdims=True)
    return jnp.where((row == 3) | (row == 4), moved - half, moved)


def left_rows(moved, row):
    h, m, l = split3(jnp.where(row == 4, 1.0, moved))
    return jnp.concatenate([h, h, m, m, h, l], 0).astype(bf16)


def right_rows(moved, row):
    h, m, l = split3(jnp.where(row == 3, 1.0, moved))
    return jnp.concatenate([h, m, h, m, l, h], 0).astype(bf16)


def centre_of(block, row):
    return jnp.where(row < 3, jnp.mean(block, axis=1, keepdims=True), 0.0)


def weights_of(left, parts, row):
    right = jnp.concatenate([right_rows(p, row) for p in parts], 1)
    exponent = lax.dot_general(
        left_rows(left, row), right, (((0,), (0,)), ((), ())), preferred_element_type=f32
    )
    return jnp.exp2(exponent)


def fold(x):
    return jnp.sum(x.reshape(-1, 8, x.shape[-1]), 0)


MOST = 2
STEP = 0.25
UNROLL = 8
GHOSTS = 64
NONE = -300.0


def each(count, body, unroll=8):
    def group(g, _):
        for u in range(unroll):
            body(g * unroll + u)
        return 0

    lax.fori_loop(0, count // unroll, group, 0)


def column_sum(x):
    return jnp.sum(fold(x), axis=0, keepdims=True)


def force_rows(v, y):
    x, qx, q = v[0:3], v[3:6], v[6:7]
    return qx * y[7:8] + x * y[6:7] - q * y[0:3] - y[3:6]


def vector_rows(moved, q):
    x = moved[0:3]
    return jnp.concatenate([x, x * q, q, jnp.ones_like(q)], 0)


def halves(v):
    return jnp.concatenate(split2(v), 0)


def join(y):
    return y[0:8] + y[8:16]


def lanes(rows):
    return jnp.concatenate([rows[c : c + 1] for c in range(3)], 1)


def routed_sum(chosen, first, rows, values):
    number = lax.broadcasted_iota(jnp.int32, (rows, chosen.shape[1]), 0) + first
    hot = jnp.where(number == chosen, 1.0, 0.0).astype(bf16)
    width = values.shape[1]
    parts = jnp.concatenate(split3(values), 1).astype(bf16)
    out = jnp.dot(hot, parts, preferred_element_type=f32)
    return out[:, :width] + out[:, width : 2 * width] + out[:, 2 * width :]


def slot_numbers(me, devices, chosen):
    local = chosen.shape[1]

    def down(x):
        return jnp.broadcast_to(x, (128, x.shape[1])).T

    def count(hit, value):
        return jnp.sum(jnp.where(hit, value, 0), axis=0, keepdims=True)

    def number(shape, axis):
        return lax.broadcasted_iota(jnp.int32, shape, axis)

    wide, tall, square = (local, local), (local, 128), (128, 128)
    column = down(chosen)
    same = jnp.concatenate([column] * (local // 128), 1) == chosen
    rank = count(same & (number(wide, 0) < number(wide, 1)), 1)
    stays = chosen == me
    shift = lax.rem(chosen - me + devices, devices)
    slot = jnp.where(stays, devices * MOST + rank, shift * MOST + rank)
    slot_down, shift_down = down(slot), down(jnp.where(stays, 0, shift))
    block, lane = number(tall, 0), number(tall, 1)
    rows = [
        count(slot_down == lane + first, block)
        for first in range(0, devices * MOST + local - devices, 128)
    ]
    come = count((shift_down == lane) & (lane > 0), 1)
    k, other = number(square, 1), number(square, 0)
    source, other_source = (lax.rem(me - x + devices, devices) for x in (k, other))
    before = count(other_source < source, down(come))
    arrive = 0
    for r in range(MOST):
        place = down(jnp.where(come > r, before + r, -1))
        arrive = arrive + count(place == k, other * MOST + r)
    return rows + [arrive]


def step_kernel(
    domains, subs, steps, send, pairs, chosen_device, send_row, pair_row,
    pos_vel, entropy_in, masses_in, final, density, outbox, inbox, state, blocks, press, entropy, masses, own_m, pair_m, r_own, r_pair, f_own, f_pair, f_sum,
    p_out, p_in, r_out, r_in, q_out, q_in, f_out, f_in, send_sem, recv_sem, move_sems, rows_out, index,
):
    local = state.shape[0]
    half = local // 2
    devices = domains * subs
    several = devices > 1
    total = local + 2 * GHOSTS
    dom = lax.axis_index("dom")
    has_low, has_high = dom > 0, dom < domains - 1
    row = lax.broadcasted_iota(jnp.int32, (8, 128), 0)

    def links(s, phase, out, into):
        def copy(side, target):
            return pltpu.make_async_remote_copy(
                src_ref=out.at[s, side],
                dst_ref=into.at[s, 1 - side],
                send_sem=send_sem.at[s, phase, side],
                recv_sem=recv_sem.at[s, phase, 1 - side],
                device_id={"dom": target},
                device_id_type=pl.DeviceIdType.MESH,
            )

        return copy(0, dom - 1), copy(1, dom + 1)

    def begin(s, phase, out, into):
        to_low, to_high = links(s, phase, out, into)
        pl.when(has_low)(to_low.start)
        pl.when(has_high)(to_high.start)

    def finish(s, phase, out, into):
        to_low, to_high = links(s, phase, out, into)

        @pl.when(has_low)
        def _():
            to_low.wait_send()
            to_high.wait_recv()

        @pl.when(has_high)
        def _():
            to_high.wait_send()
            to_low.wait_recv()

    me = dom * subs + lax.axis_index("sub")
    mesh_id = pl.DeviceIdType.MESH

    def device(k):
        there = lax.rem(me + k, devices)
        return {"dom": there // subs, "sub": lax.rem(there, subs)}

    if several:
        barrier = pltpu.get_barrier_semaphore()

        def greet(k, _):
            pl.semaphore_signal(barrier, inc=1, device_id=device(k), device_id_type=mesh_id)
            return 0

        lax.fori_loop(1, devices, greet, 0)

    for r, numbers in enumerate(slot_numbers(me, 128, chosen_device[...])):
        rows_out[r : r + 1] = numbers

    packed = blocks

    def gather(g):
        rows = pl.ds(pl.multiple_of(g * 8, 8), 8)
        for c in range(6):
            packed[rows, c, :] = pos_vel[c, rows, :]
        packed[rows, 6, :] = entropy_in[rows, :]
        packed[rows, 7, :] = masses_in[rows, :]

    each(local // 8, gather, 4)

    to_scalars = pltpu.make_async_copy(rows_out, index, move_sems.at[2])
    to_scalars.start()
    to_scalars.wait()
    slots = 128 * MOST

    def number(t):
        return index[t // 128, lax.rem(t, 128)]

    def pack(k):
        for r in range(MOST):
            outbox[k, r] = packed[number(k * MOST + r)]

    each(devices, pack)

    for side, has in ((0, has_low), (1, has_high)):

        @pl.when(jnp.logical_not(has))
        def _(side=side):
            for s in range(steps):
                p_in[s, side] = jnp.concatenate(
                    [jnp.zeros((GHOSTS, 3, 128), f32), jnp.full((GHOSTS, 1, 128), NONE, f32)], 1
                )
                for into in (r_in, q_in, f_in):
                    into[s, side] = jnp.zeros(into.shape[2:], f32)

    def copy(source, target, k):
        return pltpu.make_async_remote_copy(
            src_ref=source, dst_ref=target, send_sem=move_sems.at[0], recv_sem=move_sems.at[1],
            device_id=device(k), device_id_type=mesh_id,
        )

    if several:
        pl.semaphore_wait(barrier, devices - 1)

        def send_moving(j, _):
            k = lax.rem(j * 45, devices)
            copy(outbox.at[k], inbox.at[k], k).start()
            return 0

        lax.fori_loop(1, devices, send_moving, 0)

    def enter(i, block):
        state[i] = block
        entropy[pl.ds(i, 1), :] = block[6:7]
        masses[pl.ds(i, 1), :] = block[7:8]

    def scaled(g):
        rows = pl.ds(pl.multiple_of(g * 8, 8), 8)
        level = jnp.log2(masses[rows, :])
        for c in range(3):
            blocks[rows, c, :] = state[rows, c, :] * SCALE
            blocks[rows, 5 + c, :] = jnp.zeros((8, 128), f32)
        blocks[rows, 3, :] = level
        blocks[rows, 4, :] = level

    def own_density(i):
        block = blocks[i]
        block = features(block, centre_of(block, row), row)
        m = weights_of(block, (block,), row)
        r_own[pl.ds(i, 1), :] = column_sum(m)
        h, l = split2(m)
        own_m[i, 0:128] = h
        own_m[i, 128:256] = l

    each(half, lambda j: enter(j, packed[number(slots + j)]))
    each(half // 8, scaled, 4)
    each(half, own_density, 64)
    if several:
        everything = pl.ds(1, devices - 1)
        whole = copy(outbox.at[everything], inbox.at[everything], 1)
        whole.wait_send()
        whole.wait_recv()

    def come(j):
        slot = number(slots + half + j)
        enter(half + j, inbox[slot // MOST, lax.rem(slot, MOST)])

    each(half, come)
    each(half // 8, lambda g: scaled(half // 8 + g), 4)

    for s in range(steps):

        if s > 0:
            each(local // 8, scaled, 4)

        def pick(j):
            for side in range(2):
                p_out[s, side, j] = blocks[send[s, side * GHOSTS + j]][0:4]

        each(GHOSTS, pick)
        if domains > 1:
            begin(s, 0, p_out, p_in)

        if s == 0:
            each(local - half, lambda j: own_density(half + j), 64)
        else:
            each(local, own_density, 64)
        if domains > 1:
            finish(s, 0, p_out, p_in)

        def ghost(j):
            for side in range(2):
                block = p_in[s, side, j]
                blocks[local + side * GHOSTS + j] = jnp.concatenate(
                    [block, block[3:4], jnp.zeros((3, 128), f32)], 0
                )

        each(GHOSTS, ghost)

        def pair_density(i):
            block = blocks[i]
            centre = centre_of(block, row)
            own, first, second = (
                features(b, centre, row)
                for b in (block, blocks[pairs[s, 0, i]], blocks[pairs[s, 1, i]])
            )
            m = weights_of(own, (first, second), row)
            sums = column_sum(m)
            r_pair[pl.ds(i, 1), :] = sums[:, :128]
            r_pair[pl.ds(local + i, 1), :] = sums[:, 128:]
            back = jnp.concatenate(split2(m[:, :128] + m[:, 128:]), 1)
            back = lax.dot_general(
                jnp.ones((8, 256), bf16), back, (((1,), (1,)), ((), ())), preferred_element_type=f32
            )
            r_own[pl.ds(i, 1), :] += back[0:1]
            h, l = split2(m)
            pair_m[i, :, 0:256] = h
            pair_m[i, :, 256:512] = l

        each(local, pair_density, 64)
        chosen = jnp.concatenate([pair_row[s, 0:1], pair_row[s, 1:2]], 1)
        sent = send_row[s : s + 1, :]
        for side in range(2):
            r_out[s, side] = routed_sum(chosen, local + side * GHOSTS, GHOSTS, r_pair[...])
        for part in range(0, local, 128):
            r_own[part : part + 128] += routed_sum(chosen, part, 128, r_pair[...])
            if part == 0 and domains > 1:
                begin(s, 1, r_out, r_in)
        if domains > 1:
            finish(s, 1, r_out, r_in)
        incoming = jnp.concatenate([r_in[s, 0], r_in[s, 1]], 0)
        rho = (r_own[...] + routed_sum(sent, 0, local, incoming)) / masses[...]
        if s == steps - 1:
            density[...] = rho
        press[0:local] = entropy[...] * jnp.exp2(jnp.log2(rho) * (-1.0 / 3.0))

        def pick_press(j):
            for side in range(2):
                q_out[s, side, pl.ds(j, 1), :] = press[pl.ds(send[s, side * GHOSTS + j], 1), :]

        each(GHOSTS, pick_press)
        if domains > 1:
            begin(s, 2, q_out, q_in)

        def own_force(i):
            block = blocks[i]
            v = vector_rows(block - centre_of(block, row), press[pl.ds(i, 1), :])
            vv = halves(v)
            y = join(
                jnp.dot(jnp.concatenate([vv, vv], 1), own_m[i], preferred_element_type=f32)
            )
            f_own[pl.ds(i, 1), :] = lanes(force_rows(v, y))

        each(local, own_force, 64)
        if domains > 1:
            finish(s, 2, q_out, q_in)
        press[local : local + GHOSTS] = q_in[s, 0]
        press[local + GHOSTS : total] = q_in[s, 1]

        def pair_force(i):
            block = blocks[i]
            centre = centre_of(block, row)
            n1, n2 = pairs[s, 0, i], pairs[s, 1, i]
            vs = [
                vector_rows(b - centre, press[pl.ds(n, 1), :])
                for b, n in ((block, i), (blocks[n1], n1), (blocks[n2], n2))
            ]
            own, first, second = (halves(v) for v in vs)
            far = jnp.concatenate([first, second, first, second], 1)
            across = lax.dot_general(
                pair_m[i], far, (((1,), (1,)), ((), ())), preferred_element_type=f32
            ).T
            f_own[pl.ds(i, 1), :] += lanes(force_rows(vs[0], join(across)))
            stacked = jnp.concatenate([pair_m[i, :, 0:256], pair_m[i, :, 256:512]], 0)
            down = join(
                jnp.dot(jnp.concatenate([own, own], 1), stacked, preferred_element_type=f32)
            )
            f_pair[pl.ds(i, 1), :] = lanes(force_rows(vs[1], down[:, :128]))
            f_pair[pl.ds(local + i, 1), :] = lanes(force_rows(vs[2], down[:, 128:]))

        each(local, pair_force, 64)
        for side in range(2):
            f_out[s, side] = routed_sum(chosen, local + side * GHOSTS, GHOSTS, f_pair[...])
        for part in range(0, local, 128):
            f_own[part : part + 128] += routed_sum(chosen, part, 128, f_pair[...])
            if part == 0 and domains > 1:
                begin(s, 3, f_out, f_in)
        if domains > 1:
            finish(s, 3, f_out, f_in)
        incoming = jnp.concatenate([f_in[s, 0], f_in[s, 1]], 0)
        for part in range(0, local, 128):
            f_sum[part : part + 128] = f_own[part : part + 128] + routed_sum(sent, part, 128, incoming)

        def move(g):
            rows = pl.ds(pl.multiple_of(g * 8, 8), 8)
            gain = (STEP / SCALE) / masses[rows, :]
            for c in range(3):
                velocity = state[rows, 3 + c, :] + f_sum[rows, c * 128 : c * 128 + 128] * gain
                if s == steps - 1:
                    final[c, rows, :] = state[rows, c, :]
                    final[3 + c, rows, :] = velocity
                else:
                    state[rows, c, :] += STEP * velocity
                    state[rows, 3 + c, :] = velocity

        each(local // 8, move, 4)


def run_steps(domains, subs, chosen, send, pairs, pos_vel, entropy, masses):
    steps = send.shape[0]
    local = pos_vel.shape[1]
    devices = domains * subs
    total = local + 2 * GHOSTS
    vmem, smem = (pl.BlockSpec(memory_space=m) for m in (pltpu.VMEM, pltpu.SMEM))
    buffers = []
    for shape in ((GHOSTS, 4, 128), (GHOSTS, 128), (GHOSTS, 128), (GHOSTS, 384)):
        buffers += [pltpu.VMEM((steps, 2) + shape, f32)] * 2
    return pl.pallas_call(
        functools.partial(step_kernel, domains, subs, steps),
        name="steps",
        out_shape=[
            jax.ShapeDtypeStruct((6, local, 128), f32),
            jax.ShapeDtypeStruct((local, 128), f32),
        ],
        in_specs=[smem] * 2 + [vmem] * 6,
        out_specs=[vmem, vmem],
        scratch_shapes=[
            pltpu.VMEM((devices, MOST, 8, 128), f32),
            pltpu.VMEM((devices, MOST, 8, 128), f32),
            pltpu.VMEM((local, 8, 128), f32),
            pltpu.VMEM((total, 8, 128), f32),
            pltpu.VMEM((total, 128), f32),
            pltpu.VMEM((local, 128), f32),
            pltpu.VMEM((local, 128), f32),
            pltpu.VMEM((local, 256, 128), bf16),
            pltpu.VMEM((local, 128, 512), bf16),
            pltpu.VMEM((local, 128), f32),
            pltpu.VMEM((2 * local, 128), f32),
            pltpu.VMEM((local, 384), f32),
            pltpu.VMEM((2 * local, 384), f32),
            pltpu.VMEM((local, 384), f32),
            *buffers,
            pltpu.SemaphoreType.DMA((steps, 4, 2)),
            pltpu.SemaphoreType.DMA((steps, 4, 2)),
            pltpu.SemaphoreType.DMA((3,)),
            pltpu.VMEM((4, 128), jnp.int32),
            pltpu.SMEM((4, 128), jnp.int32),
        ],
        compiler_params=pltpu.CompilerParams(
            vmem_limit_bytes=67_000_000,
            **(dict(collective_id=1, has_side_effects=True) if devices > 1 else {}),
        ),
    )(send, pairs, chosen, send, pairs, pos_vel, entropy, masses)


def shards(pos_vel, entropy, masses, destination, ghost_send, pair_list):
    final, density = run_steps(
        lax.axis_size("dom"), lax.axis_size("sub"), destination[None, :], ghost_send,
        jnp.transpose(pair_list, (0, 2, 1)), jnp.transpose(pos_vel, (1, 0, 2)), entropy, masses,
    )
    drift = lax.pad(final[3:], jnp.float32(0.0), ((0, 3, 0), (0, 0, 0), (0, 0, 0)))
    return jnp.transpose(final + STEP * drift, (1, 0, 2)), density


def solution(mesh):
    both = ("dom", "sub")
    in_specs = (P(both, None, None), P(both, None), P(both, None), P(both), P(None, both), P(None, both, None))
    out_specs = (P(both, None, None), P(both, None))
    return jax.shard_map(shards, mesh=mesh, in_specs=in_specs, out_specs=out_specs, check_vma=False)
```
